256 devices in a mesh: seq: 32 (over x, y, core), head: 8 (over z).
Axes of the slice: x: 4, y: 4, z: 8, core: 2. Of those that a mesh axis runs over, the one named last changes fastest.
Arguments:
- hidden: bfloat16 [49152, 4096], P('seq', 'head'), may hold values from -6 to 6
- norm_gain: float32 [4096], replicated, may hold values from 0.1 to 1.9
- w_query: bfloat16 [4096, 4096], P(None, 'head'), may hold values from -0.09375 to 0.09375
- w_out: bfloat16 [4096, 4096], P('head'), may hold values from -0.5 to 0.5
- keys: bfloat16 [49152, 1024], P('seq', 'head'), may hold values from -240 to 240
- values: bfloat16 [49152, 1024], P('seq', 'head'), may hold values from -6 to 6
- cand_count: int32 [32], P('seq'), may hold values from 1 to 384, 3072 in all
- cand_pos: int32 [12288], P('seq'), may hold values from 0 to 1535, as said below
Outputs:
- slot_update: bfloat16 [12288, 4096], P('seq', 'head')
The draws below stay inside these ranges and needn't reach their ends.
Inputs may be any that keep to these rules, and one draw needn't show every extreme that they name: `cand_pos`: each shard's 384 slots hold distinct positions within that shard; its first cand_count slots are the used ones. `cand_count`: the counts sum to 3072.
All inputs are finite; a program needn't handle non-finite values. No bound on the sum of `cand_count` on one device may be relied on, other than what follows from the above.
Results may differ from the reference program's by a relative error of at most 0.019.
The reference program's roundings to bfloat16 on the way count: a program that leaves them out, or rounds other values in their place, can miss the bound.
Values may be sent and summed in bfloat16 or wider, within the bound.
No kernel may reach another device: no remote copies, remote signals or barrier semaphores. Data moves between devices by JAX's collectives and lax.ppermute only.
A program may use at most 128 MiB of HBM per device.

```python
import math
import jax
import jax.numpy as jnp
import numpy as np
from jax import lax

D = 4096
QUERY_HEADS = 32
KEY_VALUE_HEADS = 8
HEAD_SIZE = 128
SEQ_DEV = 1536
CAP = 384
ROUTED_TOTAL = 3072
SEQUENCE_TOKENS = 49152
N_SEQ = 32


def draw_keys(key, part):
    base_offset = 2.5 * jnp.clip(jax.random.normal(key, (SEQUENCE_TOKENS, KEY_VALUE_HEADS * HEAD_SIZE), jnp.float32), -6.0, 6.0)
    return base_offset.astype(jnp.bfloat16)


def draw_cand_pos(key, part):
    subkeys = jax.random.split(key, N_SEQ)

    def pick_slots(subkey):
        return jax.random.permutation(subkey, SEQ_DEV)[:CAP]
    picked = jax.vmap(pick_slots)(subkeys)
    return picked.reshape(N_SEQ * CAP).astype(jnp.int32)


def block_scale(key, shape, shards, least, high):
    def one(dim, shards_of):
        draws = jax.random.uniform(jax.random.fold_in(jax.random.fold_in(key, 6), dim), (shards_of,), jnp.float32, least / len(shards), high / len(shards))
        return jnp.repeat(jnp.exp(draws), shape[dim] // shards_of).reshape((-1,) + (1,) * (len(shape) - dim - 1))

    gain = one(*shards[0])
    for cut in shards[1:]:
        gain = gain * one(*cut)
    return gain


def split_up(number_of, total, bound, slope):
    weights = [(1 << 20) // math.isqrt(grade ** slope) + 1 for grade in range(2, number_of + 1)]
    spare, counts = total - bound - (number_of - 1), [1] * (number_of - 1)
    while spare > 0:
        movable = [i for i in range(number_of - 1) if counts[i] < bound]
        pool, remaining = sum([weights[i] for i in movable]), spare
        for i in movable:
            addition = min(bound - counts[i], max(1, remaining * weights[i] // pool), spare)
            counts[i] = counts[i] + addition
            spare = spare - addition
    return np.array([bound] + counts)


def ragged(rng, count, total, reach, skew):
    if count == 2:
        one = jax.random.randint(rng, (), max(1, total - reach), min(reach, total - 1) + 1)
        return jnp.stack([one, total - one])
    sizes = jnp.asarray(split_up(count, total, reach, skew), jnp.int32)
    couples = (count - 1) // 2
    source_of, taker = sizes[1:1 + 2 * couples:2], sizes[2:2 + 2 * couples:2]
    room = jnp.minimum(source_of - 1, reach - taker)
    shifted = jax.random.randint(jax.random.fold_in(rng, 1), (couples,), 0, 1 << 20) % (room + 1)
    sizes = sizes.at[1:1 + 2 * couples:2].set(source_of - shifted).at[2:2 + 2 * couples:2].set(taker + shifted)
    return sizes[jax.random.permutation(jax.random.fold_in(rng, 2), count)]


def gaussian(stream_key, dims, scale, most, pieces=(), held_as=jnp.bfloat16):
    array = jax.random.normal(stream_key, dims, jnp.float32) * scale
    if len(pieces) > 0:
        array = block_scale(stream_key, dims, pieces, -0.22, 0.18) * array
    return jnp.clip(array, min=-most, max=most).astype(held_as)


def setup_inputs(seed: int = 0) -> dict:
    streams_of = jax.random.split(jax.random.key(seed), 9)
    hidden = gaussian(streams_of[0], (SEQUENCE_TOKENS, D), 1.0, 6.0, ((0, 32), (1, 8)))
    norm_gain = jnp.clip(1.0 + 0.18 * jax.random.normal(streams_of[1], (D,), jnp.float32), 0.1, 1.9)
    w_query = gaussian(streams_of[2], (D, QUERY_HEADS * HEAD_SIZE), D ** -0.5, 0.09375, ((1, 8),))
    w_out = gaussian(streams_of[3], (QUERY_HEADS * HEAD_SIZE, D), HEAD_SIZE ** -0.5, 0.5, ((0, 8),))
    keys = draw_keys(jax.random.fold_in(streams_of[8], 71), 0)
    values = gaussian(streams_of[5], (SEQUENCE_TOKENS, KEY_VALUE_HEADS * HEAD_SIZE), 1.0, 6.0, ((0, 32), (1, 8)))
    cand_count = ragged(streams_of[6], N_SEQ, ROUTED_TOTAL, CAP, 2).astype(jnp.int32)
    cand_pos = draw_cand_pos(jax.random.fold_in(streams_of[8], 71), 0)
    return {"hidden": hidden, "norm_gain": norm_gain, "w_query": w_query, "w_out": w_out, "keys": keys, "values": values, "cand_count": cand_count, "cand_pos": cand_pos}


EPS = 1e-05
ROPE_BASE = 500000.0

def rotate(query_rows, positions):
    half_dim = HEAD_SIZE // 2
    inverse_freq = jnp.exp(-math.log(ROPE_BASE) * 2.0 * jnp.arange(half_dim, dtype=jnp.float32) / HEAD_SIZE)
    angles = positions.astype(jnp.float32)[:, None] * inverse_freq[None, :]
    cosine = jnp.cos(angles)[:, None, :]
    sine_part = jnp.sin(angles)[:, None, :]
    first_half = query_rows[..., :half_dim]
    second_half = query_rows[..., half_dim:]
    return jnp.concatenate([first_half * cosine - second_half * sine_part, second_half * cosine + first_half * sine_part], axis=-1)

def reference(hidden, norm_gain, w_query, w_out, keys, values, cand_count, cand_pos):
    slot_ids = jnp.arange(N_SEQ * CAP, dtype=jnp.int32)
    owner_shard = slot_ids // CAP
    within = slot_ids % CAP
    offsets = (jnp.cumsum(cand_count) - cand_count).astype(jnp.int32)
    is_live = within < cand_count[owner_shard]
    row_ids = jnp.where(is_live, offsets[owner_shard] + within, ROUTED_TOTAL).astype(jnp.int32)
    positions = (owner_shard * SEQ_DEV + cand_pos).astype(jnp.int32)
    compact_pos = jnp.zeros((ROUTED_TOTAL + 1,), jnp.int32).at[row_ids].set(positions)[:ROUTED_TOTAL]
    gathered = hidden[compact_pos].astype(jnp.float32)
    inv_rms = lax.rsqrt(lax.optimization_barrier(jnp.mean(gathered * gathered, axis=1, keepdims=True)) + EPS)
    normed = (gathered * inv_rms * norm_gain).astype(jnp.bfloat16)
    query_rows = jnp.dot(normed, w_query, preferred_element_type=jnp.float32).reshape(ROUTED_TOTAL, QUERY_HEADS, HEAD_SIZE)
    query_rows = (rotate(query_rows, compact_pos) * (1.0 / math.sqrt(HEAD_SIZE))).astype(jnp.bfloat16)
    rows_per_block = 32
    grouped_heads = query_rows.reshape(ROUTED_TOTAL // rows_per_block, rows_per_block, KEY_VALUE_HEADS, QUERY_HEADS // KEY_VALUE_HEADS, HEAD_SIZE)
    key_widened = keys.reshape(SEQUENCE_TOKENS, KEY_VALUE_HEADS, HEAD_SIZE).astype(jnp.float32)
    value_widened = values.reshape(SEQUENCE_TOKENS, KEY_VALUE_HEADS, HEAD_SIZE).astype(jnp.float32)
    key_index = jnp.arange(SEQUENCE_TOKENS, dtype=jnp.int32)

    def attend(block_item):
        block_q, block_pos = block_item
        scores = jnp.einsum('qgrd,tgd->qgrt', block_q.astype(jnp.float32), key_widened)
        visible = key_index[None, None, None, :] <= block_pos[:, None, None, None]
        scores = jnp.where(visible, scores, -jnp.inf)
        peak_row = lax.optimization_barrier(jnp.max(scores, axis=3, keepdims=True))
        weight = jnp.exp(scores - peak_row)
        denominator = lax.optimization_barrier(jnp.sum(weight, axis=3))
        rounded = lax.optimization_barrier(weight.astype(jnp.bfloat16))
        numerator = jnp.einsum('qgrt,tgd->qgrd', rounded.astype(jnp.float32), value_widened)
        return (numerator / denominator[..., None]).astype(jnp.bfloat16)
    mixed_heads = lax.map(attend, (grouped_heads, compact_pos.reshape(ROUTED_TOTAL // rows_per_block, rows_per_block)))
    mixed_heads = mixed_heads.reshape(ROUTED_TOTAL, QUERY_HEADS * HEAD_SIZE)
    update = jnp.dot(mixed_heads, w_out, preferred_element_type=jnp.float32).astype(jnp.bfloat16)
    padded = jnp.concatenate([update, jnp.zeros((1, D), jnp.bfloat16)], axis=0)
    return padded[row_ids]
```

```python
import functools
import math

import jax
import jax.numpy as jnp
from jax import lax
from jax.experimental import pallas as pl
from jax.experimental.pallas import tpu as pltpu
from jax.sharding import Mesh
from jax.sharding import PartitionSpec as P

HEAD = 128
HEADS = 4
ROWS = 128
GROUP = 16
META = 128
TILE = 32
SEQ = ("seq_0", "seq_1", "seq_2")
EPS = 1e-05
ROPE_BASE = 500000.0
NEG = -1e30
BF = jnp.bfloat16
F32 = jnp.float32
VM = pl.BlockSpec(memory_space=pltpu.VMEM)
SM = pl.BlockSpec(memory_space=pltpu.SMEM)
ANY = pl.BlockSpec(memory_space=pl.ANY)


def iota(shape, dim):
    return lax.broadcasted_iota(jnp.int32, shape, dim)


def onehot(mask):
    return jnp.where(mask, 1.0, 0.0).astype(BF)


def call(kernel, out, specs, *args, flops=0, moved=0, **kw):
    return pl.pallas_call(
        kernel,
        out_shape=out,
        in_specs=specs,
        out_specs=jax.tree.map(lambda _: VM, out),
        cost_estimate=pl.CostEstimate(flops=flops, bytes_accessed=moved, transcendentals=0),
        **kw,
    )(*args)


def pack_kernel(shards, scal, pos, hidden, out):
    s, count = scal[0], scal[1]
    slots, tokens, width = pos.shape[1], hidden.shape[0], hidden.shape[1]
    block = 128
    for b in range(shards * GROUP // block):
        o = iota((block, slots), 0) + b * block
        k = o & (GROUP - 1)
        slot = k * shards + (((o // GROUP) - s + shards) & (shards - 1))
        at = jnp.sum(
            jnp.where(iota((block, slots), 1) == slot, pos[...], 0).astype(F32),
            axis=1,
            keepdims=True,
        ).astype(jnp.int32)
        oc = iota((block, 1), 0) + b * block
        kc = oc & (GROUP - 1)
        slot_c = kc * shards + (((oc // GROUP) - s + shards) & (shards - 1))
        live = (kc < slots // shards) & (slot_c < count)
        pick = onehot((iota((block, tokens), 1) == at) & live)
        rows = slice(b * block, (b + 1) * block)
        out[rows, :width] = jnp.dot(pick, hidden[...], preferred_element_type=F32).astype(BF)
        token = at + s * tokens
        lane = iota((block, META), 1)
        meta = jnp.where(lane == 0, token // 256, jnp.where(lane == 1, token & 255, 1))
        meta = jnp.where((lane < 3) & live, meta, 0)
        out[rows, width:] = meta.astype(F32).astype(BF)


def compact_kernel(got, rows_out, meta_out, back_out):
    n = got.shape[0]
    width = got.shape[1] - META
    meta = got[:, width:]
    lower = onehot(iota((n, n), 0) >= iota((n, n), 1))
    running = jnp.dot(lower, meta, preferred_element_type=F32)[:, 2:3]
    live = meta.astype(F32)[:, 2:3]
    target = jnp.where(live > 0.5, running - 1.0, -1.0)
    back = jnp.where(iota((n, ROWS), 1).astype(F32) == target, 1.0, 0.0)
    back_out[...] = back.astype(BF)
    place = back.T.astype(BF)
    rows_out[...] = jnp.dot(place, got[:, :width], preferred_element_type=F32).astype(BF)
    meta_out[...] = jnp.dot(place, meta, preferred_element_type=F32).astype(BF)


def project_kernel(order, scal, meta, gain, cosine, sine, weight, *refs):
    xs, out = refs[:-1], refs[-1]
    width = xs[0].shape[1]
    n = len(xs)
    total = jnp.zeros((ROWS, 1), F32)
    for x in xs:
        w = x[...].astype(F32)
        total += jnp.sum(w * w, axis=1, keepdims=True)
    inv = lax.rsqrt(total / (n * width) + EPS)
    acc = jnp.zeros((ROWS, weight.shape[1]), F32)
    for delta, x in zip(order, xs):
        block = (scal[0] + delta + n) % n
        at = pl.ds(pl.multiple_of(block * width, width), width)
        normed = (x[...].astype(F32) * inv * gain[:, at]).astype(BF)
        acc += jnp.dot(normed, weight[at, :], preferred_element_type=F32)
    scale = 1.0 / math.sqrt(HEAD)
    for h in range(HEADS):
        at = slice(h * HEAD, (h + 1) * HEAD)
        part = acc[:, at]
        turned = part * cosine[...] + pltpu.roll(part, HEAD // 2, 1) * sine[...]
        out[:, at] = (turned * scale).astype(BF)
    out[:, HEADS * HEAD :] = meta[...]


def three(x):
    a = x.astype(BF).astype(F32)
    b = (x - a).astype(BF).astype(F32)
    return a, b, x - a - b


def attend_kernel(shard_ids, query, *refs):
    n = (len(refs) - 9) // 2
    keys, values = refs[:n], refs[n : 2 * n]
    out, kbuf, vbuf, qbuf, acc, peak, total, ksem, vsem = refs[2 * n :]
    tokens = keys[0].shape[0]
    for i in range(n):
        pltpu.make_async_copy(keys[i], kbuf.at[i], ksem.at[i]).start()
        pltpu.make_async_copy(values[i], vbuf.at[i], vsem.at[i]).start()
    tiles = ROWS // TILE
    big = TILE * HEADS
    meta = query[:, HEADS * HEAD :].astype(F32)
    row_pos = meta[:, 0:1] * 256.0 + meta[:, 1:2]
    live = meta[:, 2:3] > 0.5
    used = jnp.sum(jnp.where(live, 1.0, 0.0)).astype(jnp.int32)
    last_tile = (used + TILE - 1) // TILE
    for t in range(tiles):
        rows = slice(t * TILE, (t + 1) * TILE)
        for h in range(HEADS):
            qbuf[t, h * TILE : (h + 1) * TILE, :HEAD] = query[rows, h * HEAD : (h + 1) * HEAD]
            qbuf[t, h * TILE : (h + 1) * TILE, HEAD:] = query[rows, HEADS * HEAD :]
    acc[...] = jnp.zeros_like(acc)
    total[...] = jnp.zeros_like(total)
    peak[...] = jnp.full_like(peak, NEG)

    def step(i, start, masked):
        def tile(t, _):
            q = qbuf[t, :, :HEAD]
            scores = lax.dot_general(
                q, kbuf[i], (((1,), (1,)), ((), ())), preferred_element_type=F32
            )
            if masked:
                m = qbuf[t, :, HEAD:].astype(F32)
                rel = (m[:, 0:1] * 256.0 + m[:, 1:2]).astype(jnp.int32) - start
                scores = jnp.where(iota((big, tokens), 1) <= rel, scores, -jnp.inf)
            before = peak[t]
            now = jnp.maximum(before, jnp.max(scores, axis=1, keepdims=True))
            peak[t] = now
            weight = jnp.exp(scores - now[:, 0:1])
            fade = jnp.exp(before - now)
            total[t] = total[t] * fade + jnp.sum(weight, axis=1, keepdims=True)
            acc[t] = acc[t] * fade + jnp.dot(
                weight.astype(BF), vbuf[i], preferred_element_type=F32
            )
            return 0

        return tile

    def shard(i, _):
        pltpu.make_async_copy(keys[0], kbuf.at[i], ksem.at[i]).wait()
        pltpu.make_async_copy(values[0], vbuf.at[i], vsem.at[i]).wait()
        start = shard_ids[i] * tokens
        below = live & (row_pos < start.astype(F32))
        within = live & (row_pos < (start + tokens).astype(F32))
        first = jnp.sum(jnp.where(below, 1.0, 0.0)).astype(jnp.int32)
        after = jnp.sum(jnp.where(within, 1.0, 0.0)).astype(jnp.int32)
        lo = first // TILE
        mid = jnp.where(after > first, (after + TILE - 1) // TILE, (first + TILE - 1) // TILE)
        lax.fori_loop(lo, mid, step(i, start, True), 0)
        lax.fori_loop(mid, last_tile, step(i, start, False), 0)
        return 0

    lax.fori_loop(0, n, shard, 0)
    for t in range(tiles):
        rows = slice(t * TILE, (t + 1) * TILE)
        lane = iota((TILE, META), 1)
        block = jnp.zeros((TILE, META), F32)
        for h in range(HEADS):
            part = slice(h * TILE, (h + 1) * TILE)
            out[rows, h * HEAD : (h + 1) * HEAD] = acc[t, part, :].astype(BF)
            pieces = three(peak[t, part, :]) + three(total[t, part, :])
            for c, piece in enumerate(pieces):
                block = jnp.where(lane == c * HEADS + h, piece, block)
        out[rows, HEADS * HEAD :] = block.astype(BF)


def output_kernel(weight, *refs):
    parts, out = refs[:-1], refs[-1]
    peaks, totals = [], []
    for part in parts:
        meta = part[:, HEADS * HEAD :].astype(F32)
        shifted = [meta] + [pltpu.roll(meta, META - HEADS * c, 1) for c in range(1, 6)]
        peaks.append(shifted[0] + shifted[1] + shifted[2])
        totals.append(shifted[3] + shifted[4] + shifted[5])
    top = functools.reduce(jnp.maximum, peaks)
    fades = [jnp.exp(p - top) for p in peaks]
    denom = sum(f * t for f, t in zip(fades, totals))
    cols = []
    for h in range(HEADS):
        at = slice(h * HEAD, (h + 1) * HEAD)
        numer = sum(f[:, h : h + 1] * p[:, at].astype(F32) for f, p in zip(fades, parts))
        d = denom[:, h : h + 1]
        cols.append((numer / jnp.where(d > 0.0, d, 1.0)).astype(BF))
    mixed = jnp.concatenate(cols, axis=1)
    width = out.shape[2]
    for z in range(out.shape[0]):
        out[z] = jnp.dot(
            mixed, weight[:, z * width : (z + 1) * width], preferred_element_type=F32
        ).astype(BF)


def spread_kernel(back, parts, out):
    total = parts[0].astype(F32)
    for z in range(1, parts.shape[0]):
        total += parts[z].astype(F32)
    out[...] = jnp.dot(back[...], total.astype(BF), preferred_element_type=F32).astype(BF)


def unpack_kernel(shards, scal, got, out):
    s, count = scal[0], scal[1]
    slots, n = out.shape[0], got.shape[0]
    slot = iota((slots, n), 0)
    source = ((slot + s) & (shards - 1)) * GROUP + slot // shards
    pick = onehot((iota((slots, n), 1) == source) & (slot < count))
    out[...] = jnp.dot(pick, got[...], preferred_element_type=F32).astype(BF)


def shift(n, k):
    return [(i, (i + k) % n) for i in range(n)]


def body(hidden, norm_gain, w_query, w_out, keys, values, cand_count, cand_pos):
    x, y, c = (lax.axis_index(a) for a in SEQ)
    z = lax.axis_index("head")
    nx, ny, nc, nz = (lax.axis_size(a) for a in (*SEQ, "head"))
    shards = nx * ny * nc
    s = (x * ny + y) * nc + c
    slots = cand_pos.shape[0]
    width = hidden.shape[1]
    lanes = shards * GROUP
    scal = jnp.stack([s, cand_count[0]]).astype(jnp.int32)

    send = call(
        functools.partial(pack_kernel, shards),
        jax.ShapeDtypeStruct((lanes, width + META), BF),
        [SM, VM, VM],
        scal,
        cand_pos.reshape(1, slots),
        hidden,
    )
    got = lax.all_to_all(send.reshape(shards, GROUP, -1), SEQ, 0, 0, tiled=True)
    got = got.reshape(lanes, -1)

    swap = [(0, 1), (1, 0)]
    keys, values, got = lax.optimization_barrier((keys, values, got))
    k_left, v_left = (lax.ppermute(a, SEQ[0], shift(nx, 1)) for a in (keys, values))
    k_right, v_right = (lax.ppermute(a, SEQ[0], shift(nx, -1)) for a in (keys, values))
    k_far = lax.ppermute(k_left, SEQ[0], shift(nx, 1))
    v_far = lax.ppermute(v_right, SEQ[0], shift(nx, -1))
    near_k, near_v = [keys, k_left, k_right, k_far], [values, v_left, v_right, v_far]
    all_k = near_k + [lax.ppermute(a, SEQ[2], swap) for a in near_k]
    all_v = near_v + [lax.ppermute(a, SEQ[2], swap) for a in near_v]
    places = [((x + d) % nx, cc) for cc in (c, 1 - c) for d in (0, nx - 1, 1, 2)]
    shard_ids = jnp.stack([(px * ny + y) * nc + pc for px, pc in places]).astype(jnp.int32)

    rows, meta, back = call(
        compact_kernel,
        (
            jax.ShapeDtypeStruct((ROWS, width), BF),
            jax.ShapeDtypeStruct((ROWS, META), BF),
            jax.ShapeDtypeStruct((lanes, ROWS), BF),
        ),
        [VM],
        got,
    )
    up, down = rows, rows
    slices, order = [rows], [0]
    for k in range(1, nz // 2 + 1):
        up = lax.ppermute(up, "head", shift(nz, 1))
        slices.append(up)
        order.append(-k)
        if k < nz // 2:
            down = lax.ppermute(down, "head", shift(nz, -1))
            slices.append(down)
            order.append(k)

    half = HEAD // 2
    freq = jnp.exp(-math.log(ROPE_BASE) * 2.0 * jnp.arange(half, dtype=F32) / HEAD)
    meta_f = meta[:, :2].astype(F32)
    angle = (meta_f[:, 0:1] * 256.0 + meta_f[:, 1:2]) * freq[None, :]
    cosine, sine = jnp.cos(angle), jnp.sin(angle)
    cosine = jnp.concatenate([cosine, cosine], axis=1)
    sine = jnp.concatenate([-sine, sine], axis=1)

    query = call(
        functools.partial(project_kernel, tuple(order)),
        jax.ShapeDtypeStruct((ROWS, HEADS * HEAD + META), BF),
        [SM, VM, VM, VM, VM, VM] + [VM] * nz,
        z.reshape(1).astype(jnp.int32),
        meta,
        norm_gain.reshape(1, -1),
        cosine,
        sine,
        w_query,
        *slices,
    )

    tokens = keys.shape[0]
    n = len(all_k)
    big = TILE * HEADS
    tiles = ROWS // TILE

    def attend(q):
        return call(
            attend_kernel,
            jax.ShapeDtypeStruct((ROWS, HEADS * HEAD + META), BF),
            [SM, VM] + [ANY] * (2 * n),
            shard_ids,
            q,
            *all_k,
            *all_v,
            flops=5 * 10**9,
            moved=7 * 10**6,
            scratch_shapes=[
                pltpu.VMEM((n, tokens, HEAD), BF),
                pltpu.VMEM((n, tokens, HEAD), BF),
                pltpu.VMEM((tiles, big, HEAD + META), BF),
                pltpu.VMEM((tiles, big, HEAD), F32),
                pltpu.VMEM((tiles, big, HEAD), F32),
                pltpu.VMEM((tiles, big, HEAD), F32),
                pltpu.SemaphoreType.DMA((n,)),
                pltpu.SemaphoreType.DMA((n,)),
            ],
        )

    asked = [(k, lax.ppermute(query, SEQ[1], shift(ny, k))) for k in (1, ny - 1, 2)]
    parts = [attend(query)]
    for k, q in asked:
        parts.append(lax.ppermute(attend(q), SEQ[1], shift(ny, -k)))

    partial = call(
        output_kernel,
        jax.ShapeDtypeStruct((nz, ROWS, width), BF),
        [VM] * (1 + ny),
        w_out,
        *parts,
    )
    arrived = lax.all_to_all(partial, "head", 0, 0, tiled=True)
    to_send = call(
        spread_kernel, jax.ShapeDtypeStruct((lanes, width), BF), [VM, VM], back, arrived
    )
    returned = lax.all_to_all(to_send.reshape(shards, GROUP, width), SEQ, 0, 0, tiled=True)
    return call(
        functools.partial(unpack_kernel, shards),
        jax.ShapeDtypeStruct((slots, width), BF),
        [SM, VM],
        scal,
        returned.reshape(lanes, width),
    )


def solution(mesh):
    split = Mesh(
        mesh.devices.reshape(4, 4, 2, mesh.shape["head"]), ("seq_0", "seq_1", "seq_2", "head")
    )
    placed = (
        P(SEQ, "head"),
        P(),
        P(None, "head"),
        P("head", None),
        P(SEQ, "head"),
        P(SEQ, "head"),
        P(SEQ),
        P(SEQ),
    )
    return jax.shard_map(
        body, mesh=split, in_specs=placed, out_specs=P(SEQ, "head"), check_vma=False
    )
```

```python
import functools
import math

import jax
import jax.numpy as jnp
from jax import lax
from jax.experimental import pallas as pl
from jax.experimental.pallas import tpu as pltpu
from jax.sharding import Mesh
from jax.sharding import PartitionSpec as P

HEAD = 128
HEADS = 4
ROWS = 128
GROUP = 16
META = 128
TILE = 32
SEQ = ("seq_0", "seq_1", "seq_2")
EPS = 1e-05
ROPE_BASE = 500000.0
NEG = -1e30
BF = jnp.bfloat16
F32 = jnp.float32
VM = pl.BlockSpec(memory_space=pltpu.VMEM)
SM = pl.BlockSpec(memory_space=pltpu.SMEM)
ANY = pl.BlockSpec(memory_space=pl.ANY)


def iota(shape, dim):
    return lax.broadcasted_iota(jnp.int32, shape, dim)


def onehot(mask):
    return jnp.where(mask, 1.0, 0.0).astype(BF)


def call(kernel, out, specs, *args, flops=0, moved=0, **kw):
    return pl.pallas_call(
        kernel,
        out_shape=out,
        in_specs=specs,
        out_specs=jax.tree.map(lambda _: VM, out),
        cost_estimate=pl.CostEstimate(flops=flops, bytes_accessed=moved, transcendentals=0),
        **kw,
    )(*args)


def pack_kernel(shards, scal, pos, hidden, out):
    s, count = scal[0], scal[1]
    slots, tokens, width = pos.shape[1], hidden.shape[0], hidden.shape[1]
    block = 128
    for b in range(shards * GROUP // block):
        o = iota((block, slots), 0) + b * block
        k = o & (GROUP - 1)
        slot = k * shards + (((o // GROUP) - s + shards) & (shards - 1))
        at = jnp.sum(
            jnp.where(iota((block, slots), 1) == slot, pos[...], 0).astype(F32),
            axis=1,
            keepdims=True,
        ).astype(jnp.int32)
        oc = iota((block, 1), 0) + b * block
        kc = oc & (GROUP - 1)
        slot_c = kc * shards + (((oc // GROUP) - s + shards) & (shards - 1))
        live = (kc < slots // shards) & (slot_c < count)
        pick = onehot((iota((block, tokens), 1) == at) & live)
        rows = slice(b * block, (b + 1) * block)
        out[rows, :width] = jnp.dot(pick, hidden[...], preferred_element_type=F32).astype(BF)
        token = at + s * tokens
        lane = iota((block, META), 1)
        meta = jnp.where(lane == 0, token // 256, jnp.where(lane == 1, token & 255, 1))
        meta = jnp.where((lane < 3) & live, meta, 0)
        out[rows, width:] = meta.astype(F32).astype(BF)


def turn_kernel(values, out):
    out[...] = values[...].T


def compact_kernel(got, rows_out, meta_out, back_out):
    n = got.shape[0]
    width = got.shape[1] - META
    meta = got[:, width:]
    lower = onehot(iota((n, n), 0) >= iota((n, n), 1))
    running = jnp.dot(lower, meta, preferred_element_type=F32)[:, 2:3]
    live = meta.astype(F32)[:, 2:3]
    target = jnp.where(live > 0.5, running - 1.0, -1.0)
    back = jnp.where(iota((n, ROWS), 1).astype(F32) == target, 1.0, 0.0)
    back_out[...] = back.astype(BF)
    place = back.T.astype(BF)
    rows_out[...] = jnp.dot(place, got[:, :width], preferred_element_type=F32).astype(BF)
    meta_out[...] = jnp.dot(place, meta, preferred_element_type=F32).astype(BF)


def project_kernel(order, scal, meta, gain, cosine, sine, weight, *refs):
    xs, out = refs[:-1], refs[-1]
    width = xs[0].shape[1]
    n = len(xs)
    total = jnp.zeros((ROWS, 1), F32)
    for x in xs:
        w = x[...].astype(F32)
        total += jnp.sum(w * w, axis=1, keepdims=True)
    inv = lax.rsqrt(total / (n * width) + EPS)
    acc = jnp.zeros((ROWS, weight.shape[1]), F32)
    for delta, x in zip(order, xs):
        block = (scal[0] + delta + n) % n
        at = pl.ds(pl.multiple_of(block * width, width), width)
        normed = (x[...].astype(F32) * inv * gain[:, at]).astype(BF)
        acc += jnp.dot(normed, weight[at, :], preferred_element_type=F32)
    scale = 1.0 / math.sqrt(HEAD)
    for h in range(HEADS):
        at = slice(h * HEAD, (h + 1) * HEAD)
        part = acc[:, at]
        turned = part * cosine[...] + pltpu.roll(part, HEAD // 2, 1) * sine[...]
        out[:, at] = (turned * scale).astype(BF)
    out[:, HEADS * HEAD :] = meta[...]


def three(x):
    a = x.astype(BF).astype(F32)
    b = (x - a).astype(BF).astype(F32)
    return a, b, x - a - b


def attend_kernel(shard_ids, query, *refs):
    n = (len(refs) - 11) // 2
    keys, values = refs[:n], refs[n : 2 * n]
    out, kbuf, vbuf, qbuf, place, even, odd, acc, peak, steps, sem = refs[2 * n :]
    tokens = keys[0].shape[0]
    for i in range(n):
        pltpu.make_async_copy(keys[i], kbuf.at[i], sem.at[0, i]).start()
        pltpu.make_async_copy(values[i], vbuf.at[i, pl.ds(0, HEAD)], sem.at[1, i]).start()
    tiles = ROWS // TILE
    big = TILE * HEADS
    lane = iota((8, ROWS), 1)
    meta = query[:, HEADS * HEAD :].astype(F32).T
    row_pos = meta[0:1, :] * 256.0 + meta[1:2, :]
    row_pos = jnp.where(meta[2:3, :] > 0.5, row_pos, 1e9)
    used = jnp.sum(jnp.where(row_pos < 1e8, 1.0, 0.0)).astype(jnp.int32)
    last_tile = (used + TILE - 1) // TILE
    wide = jnp.broadcast_to(row_pos, (8, ROWS))
    for t in range(tiles):
        rows = slice(t * TILE, (t + 1) * TILE)
        spot = jnp.zeros((8, ROWS), F32)
        for h in range(HEADS):
            qbuf[t, h * TILE : (h + 1) * TILE, :] = query[rows, h * HEAD : (h + 1) * HEAD]
            moved = pltpu.roll(wide, (h * TILE - t * TILE) % ROWS, 1)
            spot = jnp.where((lane >= h * TILE) & (lane < (h + 1) * TILE), moved, spot)
        place[t] = spot.astype(jnp.int32)
    vbuf[:, HEAD:, :] = jnp.ones((n, vbuf.shape[1] - HEAD, tokens), BF)
    acc[...] = jnp.zeros_like(acc)
    peak[...] = jnp.full_like(peak, NEG)

    count = jnp.int32(0)
    for i in range(n):
        start = (shard_ids[i] * tokens).astype(F32)
        first = jnp.sum(jnp.where(row_pos < start, 1.0, 0.0)).astype(jnp.int32)
        for t in range(tiles):
            steps[count] = i * tiles + t
            count += ((t >= first // TILE) & (t < last_tile)).astype(jnp.int32)
    for k in range(3):
        steps[count + k] = n * tiles

    def arrive(done, upto):
        def wait(i, _):
            pltpu.make_async_copy(keys[0], kbuf.at[i], sem.at[0, i]).wait()
            pltpu.make_async_copy(values[0], vbuf.at[i, pl.ds(0, HEAD)], sem.at[1, i]).wait()
            return 0

        lax.fori_loop(done, upto, wait, 0)
        return jnp.maximum(done, upto)

    def parts(code):
        none = code >= n * tiles
        i = jnp.where(none, 0, code // tiles)
        return i, jnp.where(none, 0, code % tiles), none

    def score(code, into):
        i, t, _ = parts(code)
        into[...] = lax.dot_general(
            kbuf[i], qbuf[t], (((1,), (1,)), ((), ())), preferred_element_type=F32
        )

    def absorb(code, scores):
        i, t, none = parts(code)
        start = jnp.where(none, 1 << 30, shard_ids[i] * tokens)
        rel = place[t][0:1, :] - start
        s = jnp.where(iota((tokens, big), 0) <= rel, scores[...], -jnp.inf)
        before = peak[t][0:1, :]
        now = jnp.maximum(before, jnp.max(s, axis=0, keepdims=True))
        peak[t] = jnp.broadcast_to(now, (8, big))
        weight = jnp.exp(s - now).astype(BF)
        acc[t] = acc[t] * jnp.exp(before - now) + jnp.dot(
            vbuf[i], weight, preferred_element_type=F32
        )

    def pair(j, done):
        a, b, c = steps[2 * j], steps[2 * j + 1], steps[2 * j + 2]
        need = jnp.maximum(parts(b)[0], parts(c)[0]) + 1
        done = arrive(done, need)
        score(b, odd)
        absorb(a, even)
        score(c, even)
        absorb(b, odd)
        return done

    done = arrive(jnp.int32(0), parts(steps[0])[0] + 1)
    score(steps[0], even)
    done = lax.fori_loop(0, (count + 1) // 2, pair, done)
    arrive(done, jnp.int32(n))

    for t in range(tiles):
        rows = slice(t * TILE, (t + 1) * TILE)
        numer = acc[t, :HEAD, :].T.astype(BF)
        pieces = three(peak[t][0:1, :]) + three(acc[t, HEAD : HEAD + 1, :])
        block = jnp.zeros((META, big), F32)
        row = iota((META, big), 0)
        for k, piece in enumerate(pieces):
            block = jnp.where(row == k, piece, block)
        block = block.T
        stats = jnp.zeros((TILE, META), F32)
        for h in range(HEADS):
            out[rows, h * HEAD : (h + 1) * HEAD] = numer[h * TILE : (h + 1) * TILE, :]
            part = block[h * TILE : (h + 1) * TILE, :]
            stats += pltpu.roll(part, 8 * h, 1) if h else part
        out[rows, HEADS * HEAD :] = stats.astype(BF)


def attend(shard_ids, q, all_k, all_v):
    n = len(all_k)
    tokens = all_k[0].shape[0]
    big = TILE * HEADS
    tiles = ROWS // TILE
    return call(
        attend_kernel,
        jax.ShapeDtypeStruct((ROWS, HEADS * HEAD + META), BF),
        [SM, VM] + [ANY] * (2 * n),
        shard_ids,
        q,
        *all_k,
        *all_v,
        flops=5 * 10**9,
        moved=7 * 10**6,
        scratch_shapes=[
            pltpu.VMEM((n, tokens, HEAD), BF),
            pltpu.VMEM((n, HEAD + 16, tokens), BF),
            pltpu.VMEM((tiles, big, HEAD), BF),
            pltpu.VMEM((tiles, 8, big), jnp.int32),
            pltpu.VMEM((tokens, big), F32),
            pltpu.VMEM((tokens, big), F32),
            pltpu.VMEM((tiles, HEAD + 16, big), F32),
            pltpu.VMEM((tiles, 8, big), F32),
            pltpu.SMEM((n * tiles + 8,), jnp.int32),
            pltpu.SemaphoreType.DMA((2, n)),
        ],
    )


attend_call = attend


def output_kernel(weight, *refs):
    parts, out = refs[:-1], refs[-1]
    peaks, totals = [], []
    for part in parts:
        meta = part[:, HEADS * HEAD :].astype(F32)
        shifted = [meta] + [pltpu.roll(meta, META - c, 1) for c in range(1, 6)]
        peaks.append(shifted[0] + shifted[1] + shifted[2])
        totals.append(shifted[3] + shifted[4] + shifted[5])
    top = functools.reduce(jnp.maximum, peaks)
    fades = [jnp.exp(p - top) for p in peaks]
    denom = sum(f * t for f, t in zip(fades, totals))
    cols = []
    for h in range(HEADS):
        at = slice(h * HEAD, (h + 1) * HEAD)
        col = slice(8 * h, 8 * h + 1)
        numer = sum(f[:, col] * p[:, at].astype(F32) for f, p in zip(fades, parts))
        d = denom[:, col]
        cols.append((numer / jnp.where(d > 0.0, d, 1.0)).astype(BF))
    mixed = jnp.concatenate(cols, axis=1)
    width = out.shape[2]
    for z in range(out.shape[0]):
        out[z] = jnp.dot(
            mixed, weight[:, z * width : (z + 1) * width], preferred_element_type=F32
        ).astype(BF)


def spread_kernel(back, parts, out):
    total = parts[0].astype(F32)
    for z in range(1, parts.shape[0]):
        total += parts[z].astype(F32)
    out[...] = jnp.dot(back[...], total.astype(BF), preferred_element_type=F32).astype(BF)


def unpack_kernel(shards, scal, got, out):
    s, count = scal[0], scal[1]
    slots, n = out.shape[0], got.shape[0]
    slot = iota((slots, n), 0)
    source = ((slot + s) & (shards - 1)) * GROUP + slot // shards
    pick = onehot((iota((slots, n), 1) == source) & (slot < count))
    out[...] = jnp.dot(pick, got[...], preferred_element_type=F32).astype(BF)


def shift(n, k):
    return [(i, (i + k) % n) for i in range(n)]


def body(hidden, norm_gain, w_query, w_out, keys, values, cand_count, cand_pos):
    x, y, c = (lax.axis_index(a) for a in SEQ)
    z = lax.axis_index("head")
    nx, ny, nc, nz = (lax.axis_size(a) for a in (*SEQ, "head"))
    shards = nx * ny * nc
    s = (x * ny + y) * nc + c
    slots = cand_pos.shape[0]
    width = hidden.shape[1]
    lanes = shards * GROUP
    scal = jnp.stack([s, cand_count[0]]).astype(jnp.int32)

    send = call(
        functools.partial(pack_kernel, shards),
        jax.ShapeDtypeStruct((lanes, width + META), BF),
        [SM, VM, VM],
        scal,
        cand_pos.reshape(1, slots),
        hidden,
    )
    got = lax.all_to_all(send.reshape(shards, GROUP, -1), SEQ, 0, 0, tiled=True)
    got = got.reshape(lanes, -1)

    swap = [(0, 1), (1, 0)]
    values = call(turn_kernel, jax.ShapeDtypeStruct(values.shape[::-1], BF), [VM], values)
    keys, values, got = lax.optimization_barrier((keys, values, got))
    k_left, v_left = (lax.ppermute(a, SEQ[0], shift(nx, 1)) for a in (keys, values))
    k_right, v_right = (lax.ppermute(a, SEQ[0], shift(nx, -1)) for a in (keys, values))
    k_far = lax.ppermute(k_left, SEQ[0], shift(nx, 1))
    v_far = lax.ppermute(v_right, SEQ[0], shift(nx, -1))
    near_k, near_v = [keys, k_left, k_right, k_far], [values, v_left, v_right, v_far]
    all_k = near_k + [lax.ppermute(a, SEQ[2], swap) for a in near_k]
    all_v = near_v + [lax.ppermute(a, SEQ[2], swap) for a in near_v]
    places = [((x + d) % nx, cc) for cc in (c, 1 - c) for d in (0, nx - 1, 1, 2)]
    shard_ids = jnp.stack([(px * ny + y) * nc + pc for px, pc in places]).astype(jnp.int32)

    rows, meta, back = call(
        compact_kernel,
        (
            jax.ShapeDtypeStruct((ROWS, width), BF),
            jax.ShapeDtypeStruct((ROWS, META), BF),
            jax.ShapeDtypeStruct((lanes, ROWS), BF),
        ),
        [VM],
        got,
    )
    up, down = rows, rows
    slices, order = [rows], [0]
    for k in range(1, nz // 2 + 1):
        up = lax.ppermute(up, "head", shift(nz, 1))
        slices.append(up)
        order.append(-k)
        if k < nz // 2:
            down = lax.ppermute(down, "head", shift(nz, -1))
            slices.append(down)
            order.append(k)

    half = HEAD // 2
    freq = jnp.exp(-math.log(ROPE_BASE) * 2.0 * jnp.arange(half, dtype=F32) / HEAD)
    meta_f = meta[:, :2].astype(F32)
    angle = (meta_f[:, 0:1] * 256.0 + meta_f[:, 1:2]) * freq[None, :]
    cosine, sine = jnp.cos(angle), jnp.sin(angle)
    cosine = jnp.concatenate([cosine, cosine], axis=1)
    sine = jnp.concatenate([-sine, sine], axis=1)

    query = call(
        functools.partial(project_kernel, tuple(order)),
        jax.ShapeDtypeStruct((ROWS, HEADS * HEAD + META), BF),
        [SM, VM, VM, VM, VM, VM] + [VM] * nz,
        z.reshape(1).astype(jnp.int32),
        meta,
        norm_gain.reshape(1, -1),
        cosine,
        sine,
        w_query,
        *slices,
    )

    asked = [(k, lax.ppermute(query, SEQ[1], shift(ny, k))) for k in (1, ny - 1, 2)]
    parts = [attend(shard_ids, query, all_k, all_v)]
    for k, q in asked:
        parts.append(lax.ppermute(attend(shard_ids, q, all_k, all_v), SEQ[1], shift(ny, -k)))

    partial = call(
        output_kernel,
        jax.ShapeDtypeStruct((nz, ROWS, width), BF),
        [VM] * (1 + ny),
        w_out,
        *parts,
    )
    arrived = lax.all_to_all(partial, "head", 0, 0, tiled=True)
    to_send = call(
        spread_kernel, jax.ShapeDtypeStruct((lanes, width), BF), [VM, VM], back, arrived
    )
    returned = lax.all_to_all(to_send.reshape(shards, GROUP, width), SEQ, 0, 0, tiled=True)
    return call(
        functools.partial(unpack_kernel, shards),
        jax.ShapeDtypeStruct((slots, width), BF),
        [SM, VM],
        scal,
        returned.reshape(lanes, width),
    )


def solution(mesh):
    split = Mesh(
        mesh.devices.reshape(4, 4, 2, mesh.shape["head"]), ("seq_0", "seq_1", "seq_2", "head")
    )
    placed = (
        P(SEQ, "head"),
        P(),
        P(None, "head"),
        P("head", None),
        P(SEQ, "head"),
        P(SEQ, "head"),
        P(SEQ),
        P(SEQ),
    )
    return jax.shard_map(
        body, mesh=split, in_specs=placed, out_specs=P(SEQ, "head"), check_vma=False
    )
```

```python
import functools
import math

import jax
import jax.numpy as jnp
from jax import lax
from jax.experimental import pallas as pl
from jax.experimental.pallas import tpu as pltpu
from jax.sharding import Mesh
from jax.sharding import PartitionSpec as P

HEAD = 128
HEADS = 4
ROWS = 128
GROUP = 16
META = 128
TILE = 32
SEQ = ("seq_0", "seq_1", "seq_2")
EPS = 1e-05
ROPE_BASE = 500000.0
NEG = -1e30
BF = jnp.bfloat16
F32 = jnp.float32
VM = pl.BlockSpec(memory_space=pltpu.VMEM)
SM = pl.BlockSpec(memory_space=pltpu.SMEM)
ANY = pl.BlockSpec(memory_space=pl.ANY)
HB = pl.BlockSpec(memory_space=pltpu.HBM)


def iota(shape, dim):
    return lax.broadcasted_iota(jnp.int32, shape, dim)


def onehot(mask):
    return jnp.where(mask, 1.0, 0.0).astype(BF)


def call(kernel, out, specs, *args, flops=0, moved=0, limit=20, **kw):
    return pl.pallas_call(
        kernel,
        out_shape=out,
        in_specs=specs,
        out_specs=jax.tree.map(lambda _: VM, out),
        cost_estimate=pl.CostEstimate(flops=flops, bytes_accessed=moved, transcendentals=0),
        compiler_params=pltpu.CompilerParams(vmem_limit_bytes=limit << 20),
        **kw,
    )(*args)


def seq_place():
    place = jnp.int32(0)
    for a in SEQ:
        place = place * lax.axis_size(a) + lax.axis_index(a)
    return place


def pack_kernel(shards, count, pos, hidden, out):
    s, count = seq_place(), count[0]
    slots, tokens, width = pos.shape[0], hidden.shape[0], hidden.shape[1]
    where = pos[...].reshape(1, slots)
    block = 128
    for b in range(shards * GROUP // block):
        o = iota((block, slots), 0) + b * block
        k = o & (GROUP - 1)
        slot = k * shards + (((o // GROUP) - s + shards) & (shards - 1))
        at = jnp.sum(
            jnp.where(iota((block, slots), 1) == slot, where, 0).astype(F32),
            axis=1,
            keepdims=True,
        ).astype(jnp.int32)
        oc = iota((block, 1), 0) + b * block
        kc = oc & (GROUP - 1)
        slot_c = kc * shards + (((oc // GROUP) - s + shards) & (shards - 1))
        live = (kc < slots // shards) & (slot_c < count)
        pick = onehot((iota((block, tokens), 1) == at) & live)
        rows = slice(b * block, (b + 1) * block)
        out[rows, :width] = jnp.dot(pick, hidden[...], preferred_element_type=F32).astype(BF)
        token = at + s * tokens
        lane = iota((block, META), 1)
        meta = jnp.where(lane == 0, token // 256, jnp.where(lane == 1, token & 255, 1))
        meta = jnp.where((lane < 3) & live, meta, 0)
        out[rows, width:] = meta.astype(F32).astype(BF)


def turn_kernel(values, out):
    out[...] = values[...].T


def compact_kernel(got, rows_out, meta_out, back_out):
    n = got.shape[0]
    width = got.shape[1] - META
    meta = got[:, width:]
    lower = onehot(iota((n, n), 0) >= iota((n, n), 1))
    running = jnp.dot(lower, meta, preferred_element_type=F32)[:, 2:3]
    live = meta.astype(F32)[:, 2:3]
    target = jnp.where(live > 0.5, running - 1.0, -1.0)
    back = jnp.where(iota((n, ROWS), 1).astype(F32) == target, 1.0, 0.0)
    back_out[...] = back.astype(BF)
    place = back.T.astype(BF)
    rows_out[...] = jnp.dot(place, got[:, :width], preferred_element_type=F32).astype(BF)
    meta_out[...] = jnp.dot(place, meta, preferred_element_type=F32).astype(BF)


def project_kernel(order, z, meta, gain, cosine, sine, weight, *refs):
    xs, (out, held, sem) = refs[:-3], refs[-3:]
    width = xs[0].shape[1]
    n = len(xs)
    spots = []
    for k, delta in enumerate(order):
        block = (z[0] + delta + n) & (n - 1)
        at = pl.ds(pl.multiple_of(block * width, width), width)
        pltpu.make_async_copy(weight.at[at], held.at[k], sem.at[k]).start()
        spots.append(at)
    total = jnp.zeros((ROWS, 1), F32)
    for x in xs:
        w = x[...].astype(F32)
        total += jnp.sum(w * w, axis=1, keepdims=True)
    inv = lax.rsqrt(total / (n * width) + EPS)
    acc = jnp.zeros((ROWS, weight.shape[1]), F32)
    for k, x in enumerate(xs):
        normed = (x[...].astype(F32) * inv * gain[:, spots[k]]).astype(BF)
        pltpu.make_async_copy(weight.at[spots[k]], held.at[k], sem.at[k]).wait()
        acc += jnp.dot(normed, held[k], preferred_element_type=F32)
    scale = 1.0 / math.sqrt(HEAD)
    for h in range(HEADS):
        at = slice(h * HEAD, (h + 1) * HEAD)
        part = acc[:, at]
        turned = part * cosine[...] + pltpu.roll(part, HEAD // 2, 1) * sine[...]
        out[:, at] = (turned * scale).astype(BF)
    out[:, HEADS * HEAD :] = meta[...]


def three(x):
    a = x.astype(BF).astype(F32)
    b = (x - a).astype(BF).astype(F32)
    return a, b, x - a - b


def collect_kernel(*refs):
    n = (len(refs) - 3) // 2
    keys, values = refs[:n], refs[n : 2 * n]
    kbuf, vbuf, sem = refs[2 * n :]
    copies = []
    for i in range(n):
        copies.append(pltpu.make_async_copy(keys[i], kbuf.at[i], sem.at[0, i]))
        copies.append(
            pltpu.make_async_copy(values[i], vbuf.at[i, pl.ds(0, HEAD)], sem.at[1, i])
        )
    for copy in copies:
        copy.start()
    vbuf[:, HEAD:, :] = jnp.ones((n, vbuf.shape[1] - HEAD, vbuf.shape[2]), BF)
    for copy in copies:
        copy.wait()


def collect(all_k, all_v):
    n = len(all_k)
    tokens = all_k[0].shape[0]
    return call(
        collect_kernel,
        (
            jax.ShapeDtypeStruct((n, tokens, HEAD), BF),
            jax.ShapeDtypeStruct((n, HEAD + 16, tokens), BF),
        ),
        [ANY] * (2 * n),
        *all_k,
        *all_v,
        scratch_shapes=[pltpu.SemaphoreType.DMA((2, n))],
    )


def attend_kernel(
    shard_ids, query, kbuf, vbuf, out, qbuf, place, even, odd, acc, peak, steps
):
    n, tokens = kbuf.shape[0], kbuf.shape[1]
    tiles = ROWS // TILE
    big = TILE * HEADS
    lane = iota((8, ROWS), 1)
    meta = query[:, HEADS * HEAD :].astype(F32).T
    row_pos = meta[0:1, :] * 256.0 + meta[1:2, :]
    row_pos = jnp.where(meta[2:3, :] > 0.5, row_pos, 1e9)
    used = jnp.sum(jnp.where(row_pos < 1e8, 1.0, 0.0)).astype(jnp.int32)
    last_tile = (used + TILE - 1) // TILE
    wide = jnp.broadcast_to(row_pos, (8, ROWS))
    for t in range(tiles):
        rows = slice(t * TILE, (t + 1) * TILE)
        spot = jnp.zeros((8, ROWS), F32)
        for h in range(HEADS):
            qbuf[t, h * TILE : (h + 1) * TILE, :] = query[rows, h * HEAD : (h + 1) * HEAD]
            moved = pltpu.roll(wide, (h * TILE - t * TILE) % ROWS, 1)
            spot = jnp.where((lane >= h * TILE) & (lane < (h + 1) * TILE), moved, spot)
        place[t] = spot.astype(jnp.int32)
    acc[...] = jnp.zeros_like(acc)
    peak[...] = jnp.full_like(peak, NEG)

    count = jnp.int32(0)
    for i in range(n):
        start = (shard_ids[i] * tokens).astype(F32)
        first = jnp.sum(jnp.where(row_pos < start, 1.0, 0.0)).astype(jnp.int32)
        for t in range(tiles):
            steps[count] = i * tiles + t
            count += ((t >= first // TILE) & (t < last_tile)).astype(jnp.int32)
    for k in range(3):
        steps[count + k] = n * tiles

    def parts(code):
        none = code >= n * tiles
        i = jnp.where(none, 0, code // tiles)
        return i, jnp.where(none, 0, code % tiles), none

    def score(code, into):
        i, t, _ = parts(code)
        into[...] = lax.dot_general(
            kbuf[i], qbuf[t], (((1,), (1,)), ((), ())), preferred_element_type=F32
        )

    def absorb(code, scores):
        i, t, none = parts(code)
        start = jnp.where(none, 1 << 30, shard_ids[i] * tokens)
        rel = place[t][0:1, :] - start
        s = jnp.where(iota((tokens, big), 0) <= rel, scores[...], -jnp.inf)
        before = peak[t][0:1, :]
        now = jnp.maximum(before, jnp.max(s, axis=0, keepdims=True))
        peak[t] = jnp.broadcast_to(now, (8, big))
        weight = jnp.exp(s - now).astype(BF)
        acc[t] = acc[t] * jnp.exp(before - now) + jnp.dot(
            vbuf[i], weight, preferred_element_type=F32
        )

    def pair(j, _):
        a, b, c = steps[2 * j], steps[2 * j + 1], steps[2 * j + 2]
        score(b, odd)
        absorb(a, even)
        score(c, even)
        absorb(b, odd)
        return 0

    score(steps[0], even)
    lax.fori_loop(0, (count + 1) // 2, pair, 0)

    for t in range(tiles):
        rows = slice(t * TILE, (t + 1) * TILE)
        numer = acc[t, :HEAD, :].T.astype(BF)
        pieces = three(peak[t][0:1, :]) + three(acc[t, HEAD : HEAD + 1, :])
        block = jnp.zeros((META, big), F32)
        row = iota((META, big), 0)
        for k, piece in enumerate(pieces):
            block = jnp.where(row == k, piece, block)
        block = block.T
        stats = jnp.zeros((TILE, META), F32)
        for h in range(HEADS):
            out[rows, h * HEAD : (h + 1) * HEAD] = numer[h * TILE : (h + 1) * TILE, :]
            part = block[h * TILE : (h + 1) * TILE, :]
            stats += pltpu.roll(part, 8 * h, 1) if h else part
        out[rows, HEADS * HEAD :] = stats.astype(BF)


def attend(shard_ids, q, kbuf, vbuf):
    n, tokens = kbuf.shape[0], kbuf.shape[1]
    big = TILE * HEADS
    tiles = ROWS // TILE
    return call(
        attend_kernel,
        jax.ShapeDtypeStruct((ROWS, HEADS * HEAD + META), BF),
        [SM, VM, VM, VM],
        shard_ids,
        q,
        kbuf,
        vbuf,
        flops=5 * 10**9,
        moved=7 * 10**6,
        scratch_shapes=[
            pltpu.VMEM((tiles, big, HEAD), BF),
            pltpu.VMEM((tiles, 8, big), jnp.int32),
            pltpu.VMEM((tokens, big), F32),
            pltpu.VMEM((tokens, big), F32),
            pltpu.VMEM((tiles, HEAD + 16, big), F32),
            pltpu.VMEM((tiles, 8, big), F32),
            pltpu.SMEM((n * tiles + 8,), jnp.int32),
        ],
    )


def output_kernel(weight, *refs):
    parts, out = refs[:-1], refs[-1]
    peaks, totals = [], []
    for part in parts:
        meta = part[:, HEADS * HEAD :].astype(F32)
        shifted = [meta] + [pltpu.roll(meta, META - c, 1) for c in range(1, 6)]
        peaks.append(shifted[0] + shifted[1] + shifted[2])
        totals.append(shifted[3] + shifted[4] + shifted[5])
    top = functools.reduce(jnp.maximum, peaks)
    fades = [jnp.exp(p - top) for p in peaks]
    denom = sum(f * t for f, t in zip(fades, totals))
    cols = []
    for h in range(HEADS):
        at = slice(h * HEAD, (h + 1) * HEAD)
        col = slice(8 * h, 8 * h + 1)
        numer = sum(f[:, col] * p[:, at].astype(F32) for f, p in zip(fades, parts))
        d = denom[:, col]
        cols.append((numer / jnp.where(d > 0.0, d, 1.0)).astype(BF))
    mixed = jnp.concatenate(cols, axis=1)
    width = out.shape[2]
    for z in range(out.shape[0]):
        out[z] = jnp.dot(
            mixed, weight[:, z * width : (z + 1) * width], preferred_element_type=F32
        ).astype(BF)


def spread_kernel(back, parts, out):
    total = parts[0].astype(F32)
    for z in range(1, parts.shape[0]):
        total += parts[z].astype(F32)
    out[...] = jnp.dot(back[...], total.astype(BF), preferred_element_type=F32).astype(BF)


def unpack_kernel(shards, count, got, out):
    s, count = seq_place(), count[0]
    slots, n = out.shape[0], got.shape[0]
    slot = iota((slots, n), 0)
    source = ((slot + s) & (shards - 1)) * GROUP + slot // shards
    pick = onehot((iota((slots, n), 1) == source) & (slot < count))
    out[...] = jnp.dot(pick, got[...], preferred_element_type=F32).astype(BF)


def shift(n, k):
    return [(i, (i + k) % n) for i in range(n)]


def body(hidden, norm_gain, w_query, w_out, keys, values, cand_count, cand_pos):
    x, y, c = (lax.axis_index(a) for a in SEQ)
    z = lax.axis_index("head")
    nx, ny, nc, nz = (lax.axis_size(a) for a in (*SEQ, "head"))
    shards = nx * ny * nc
    s = (x * ny + y) * nc + c
    slots = cand_pos.shape[0]
    width = hidden.shape[1]
    lanes = shards * GROUP

    send = call(
        functools.partial(pack_kernel, shards),
        jax.ShapeDtypeStruct((lanes, width + META), BF),
        [SM, VM, VM],
        cand_count,
        cand_pos,
        hidden,
    )
    swap = [(0, 1), (1, 0)]
    keys, values, send = lax.optimization_barrier((keys, values, send))
    values = call(turn_kernel, jax.ShapeDtypeStruct(values.shape[::-1], BF), [VM], values)
    got = lax.all_to_all(send.reshape(shards, GROUP, -1), SEQ, 0, 0, tiled=True)
    got = got.reshape(lanes, -1)
    k_left, v_left = (lax.ppermute(a, SEQ[0], shift(nx, 1)) for a in (keys, values))
    k_right, v_right = (lax.ppermute(a, SEQ[0], shift(nx, -1)) for a in (keys, values))
    k_far = lax.ppermute(k_left, SEQ[0], shift(nx, 1))
    v_far = lax.ppermute(v_right, SEQ[0], shift(nx, -1))
    near_k, near_v = [keys, k_left, k_right, k_far], [values, v_left, v_right, v_far]
    all_k = near_k + [lax.ppermute(a, SEQ[2], swap) for a in near_k]
    all_v = near_v + [lax.ppermute(a, SEQ[2], swap) for a in near_v]
    places = [((x + d) % nx, cc) for cc in (c, 1 - c) for d in (0, nx - 1, 1, 2)]
    shard_ids = jnp.stack([(px * ny + y) * nc + pc for px, pc in places]).astype(jnp.int32)

    rows, meta, back = call(
        compact_kernel,
        (
            jax.ShapeDtypeStruct((ROWS, width), BF),
            jax.ShapeDtypeStruct((ROWS, META), BF),
            jax.ShapeDtypeStruct((lanes, ROWS), BF),
        ),
        [VM],
        got,
        flops=5 * 10**9,
        moved=10**6,
    )
    up, down = rows, rows
    slices, order = [rows], [0]
    for k in range(1, nz // 2 + 1):
        up = lax.ppermute(up, "head", shift(nz, 1))
        slices.append(up)
        order.append(-k)
        if k < nz // 2:
            down = lax.ppermute(down, "head", shift(nz, -1))
            slices.append(down)
            order.append(k)

    half = HEAD // 2
    freq = jnp.exp(-math.log(ROPE_BASE) * 2.0 * jnp.arange(half, dtype=F32) / HEAD)
    meta_f = meta[:, :2].astype(F32)
    angle = (meta_f[:, 0:1] * 256.0 + meta_f[:, 1:2]) * freq[None, :]
    cosine, sine = jnp.cos(angle), jnp.sin(angle)
    cosine = jnp.concatenate([cosine, cosine], axis=1)
    sine = jnp.concatenate([-sine, sine], axis=1)

    query = call(
        functools.partial(project_kernel, tuple(order)),
        jax.ShapeDtypeStruct((ROWS, HEADS * HEAD + META), BF),
        [SM, VM, VM, VM, VM, HB] + [VM] * nz,
        z.reshape(1).astype(jnp.int32),
        meta,
        norm_gain.reshape(1, -1),
        cosine,
        sine,
        w_query,
        *slices,
        scratch_shapes=[
            pltpu.VMEM((nz, width, w_query.shape[1]), BF),
            pltpu.SemaphoreType.DMA((nz,)),
        ],
    )

    asked = [(k, lax.ppermute(query, SEQ[1], shift(ny, k))) for k in (1, ny - 1, 2)]
    kbuf, vbuf = collect(all_k, all_v)
    last = attend(shard_ids, query, kbuf, vbuf)
    parts = [last]
    for k, q in asked:
        q, last = lax.optimization_barrier((q, last))
        last = attend(shard_ids, q, kbuf, vbuf)
        parts.append(lax.ppermute(last, SEQ[1], shift(ny, -k)))

    partial = call(
        output_kernel,
        jax.ShapeDtypeStruct((nz, ROWS, width), BF),
        [VM] * (1 + ny),
        w_out,
        *parts,
    )
    arrived = lax.all_to_all(partial, "head", 0, 0, tiled=True)
    to_send = call(
        spread_kernel, jax.ShapeDtypeStruct((lanes, width), BF), [VM, VM], back, arrived
    )
    returned = lax.all_to_all(to_send.reshape(shards, GROUP, width), SEQ, 0, 0, tiled=True)
    return call(
        functools.partial(unpack_kernel, shards),
        jax.ShapeDtypeStruct((slots, width), BF),
        [SM, VM],
        cand_count,
        returned.reshape(lanes, width),
    )


def solution(mesh):
    split = Mesh(
        mesh.devices.reshape(4, 4, 2, mesh.shape["head"]), ("seq_0", "seq_1", "seq_2", "head")
    )
    placed = (
        P(SEQ, "head"),
        P(),
        P(None, "head"),
        P("head", None),
        P(SEQ, "head"),
        P(SEQ, "head"),
        P(SEQ),
        P(SEQ),
    )
    return jax.shard_map(
        body, mesh=split, in_specs=placed, out_specs=P(SEQ, "head"), check_vma=False
    )
```

```python
import functools
import math

import jax
import jax.numpy as jnp
from jax import lax
from jax.experimental import pallas as pl
from jax.experimental.pallas import tpu as pltpu
from jax.sharding import Mesh
from jax.sharding import PartitionSpec as P

HEAD = 128
HEADS = 4
ROWS = 128
GROUP = 16
META = 128
TILE = 32
SEQ = ("seq_0", "seq_1", "seq_2")
EPS = 1e-05
ROPE_BASE = 500000.0
NEG = -1e30
BF = jnp.bfloat16
F32 = jnp.float32
VM = pl.BlockSpec(memory_space=pltpu.VMEM)
SM = pl.BlockSpec(memory_space=pltpu.SMEM)
ANY = pl.BlockSpec(memory_space=pl.ANY)
HB = pl.BlockSpec(memory_space=pltpu.HBM)


def iota(shape, dim):
    return lax.broadcasted_iota(jnp.int32, shape, dim)


def onehot(mask):
    return jnp.where(mask, 1.0, 0.0).astype(BF)


def call(kernel, out, specs, *args, flops=0, moved=0, limit=20, **kw):
    return pl.pallas_call(
        kernel,
        out_shape=out,
        in_specs=specs,
        out_specs=jax.tree.map(lambda _: VM, out),
        cost_estimate=pl.CostEstimate(flops=flops, bytes_accessed=moved, transcendentals=0),
        compiler_params=pltpu.CompilerParams(vmem_limit_bytes=limit << 20),
        **kw,
    )(*args)


def seq_place():
    place = jnp.int32(0)
    for a in SEQ:
        place = place * lax.axis_size(a) + lax.axis_index(a)
    return place


def pack_kernel(shards, count, pos, hidden, out):
    s, count = seq_place(), count[0]
    slots, tokens, width = pos.shape[0], hidden.shape[0], hidden.shape[1]
    where = pos[...].reshape(1, slots)
    block = 128
    for b in range(shards * GROUP // block):
        o = iota((block, slots), 0) + b * block
        k = o & (GROUP - 1)
        slot = k * shards + (((o // GROUP) - s + shards) & (shards - 1))
        at = jnp.sum(
            jnp.where(iota((block, slots), 1) == slot, where, 0).astype(F32),
            axis=1,
            keepdims=True,
        ).astype(jnp.int32)
        oc = iota((block, 1), 0) + b * block
        kc = oc & (GROUP - 1)
        slot_c = kc * shards + (((oc // GROUP) - s + shards) & (shards - 1))
        live = (kc < slots // shards) & (slot_c < count)
        pick = onehot((iota((block, tokens), 1) == at) & live)
        rows = slice(b * block, (b + 1) * block)
        out[rows, :width] = jnp.dot(pick, hidden[...], preferred_element_type=F32).astype(BF)
        token = at + s * tokens
        lane = iota((block, META), 1)
        meta = jnp.where(lane == 0, token // 256, jnp.where(lane == 1, token & 255, 1))
        meta = jnp.where((lane < 3) & live, meta, 0)
        out[rows, width:] = meta.astype(F32).astype(BF)


def turn_kernel(values, out):
    out[...] = values[...].T


def compact_kernel(got, rows_out, meta_out, back_out):
    n = got.shape[0]
    width = got.shape[1] - META
    meta = got[:, width:]
    lower = onehot(iota((n, n), 0) >= iota((n, n), 1))
    running = jnp.dot(lower, meta, preferred_element_type=F32)[:, 2:3]
    live = meta.astype(F32)[:, 2:3]
    spare = ROWS - running[n - 1 : n, :]
    target = jnp.where(live > 0.5, running - 1.0 + spare, -1.0)
    back = jnp.where(iota((n, ROWS), 1).astype(F32) == target, 1.0, 0.0)
    back_out[...] = back.astype(BF)
    place = back.T.astype(BF)
    rows_out[...] = jnp.dot(place, got[:, :width], preferred_element_type=F32).astype(BF)
    meta_out[...] = jnp.dot(place, meta, preferred_element_type=F32).astype(BF)


def project_kernel(order, z, meta, gain, cosine, sine, weight, *refs):
    sources, (out, held, xs, sem, xsem) = refs[:-5], refs[-5:]
    width = xs.shape[2]
    n = len(sources)
    for k, x in enumerate(sources):
        pltpu.make_async_copy(x, xs.at[k], xsem.at[k]).start()
    spots = []
    for k, delta in enumerate(order):
        block = (z[0] + delta + n) & (n - 1)
        at = pl.ds(pl.multiple_of(block * width, width), width)
        pltpu.make_async_copy(weight.at[at], held.at[k], sem.at[k]).start()
        spots.append(at)
    total = jnp.zeros((ROWS, 1), F32)
    for k, x in enumerate(sources):
        pltpu.make_async_copy(x, xs.at[k], xsem.at[k]).wait()
        w = xs[k].astype(F32)
        total += jnp.sum(w * w, axis=1, keepdims=True)
    inv = lax.rsqrt(total / (n * width) + EPS)
    acc = jnp.zeros((ROWS, weight.shape[1]), F32)
    for k in range(n):
        normed = (xs[k].astype(F32) * inv * gain[:, spots[k]]).astype(BF)
        pltpu.make_async_copy(weight.at[spots[k]], held.at[k], sem.at[k]).wait()
        acc += jnp.dot(normed, held[k], preferred_element_type=F32)
    scale = 1.0 / math.sqrt(HEAD)
    for h in range(HEADS):
        at = slice(h * HEAD, (h + 1) * HEAD)
        part = acc[:, at]
        turned = part * cosine[...] + pltpu.roll(part, HEAD // 2, 1) * sine[...]
        out[:, at] = (turned * scale).astype(BF)
    out[:, HEADS * HEAD :] = meta[...]


def three(x):
    a = x.astype(BF).astype(F32)
    b = (x - a).astype(BF).astype(F32)
    return a, b, x - a - b


def collect_kernel(*refs):
    n = (len(refs) - 3) // 2
    keys, values = refs[:n], refs[n : 2 * n]
    kbuf, vbuf, sem = refs[2 * n :]
    copies = []
    for i in range(n):
        copies.append(pltpu.make_async_copy(keys[i], kbuf.at[i], sem.at[0, i]))
        copies.append(
            pltpu.make_async_copy(values[i], vbuf.at[i, pl.ds(0, HEAD)], sem.at[1, i])
        )
    for copy in copies:
        copy.start()
    vbuf[:, HEAD:, :] = jnp.ones((n, vbuf.shape[1] - HEAD, vbuf.shape[2]), BF)
    for copy in copies:
        copy.wait()


def collect(all_k, all_v):
    n = len(all_k)
    tokens = all_k[0].shape[0]
    return call(
        collect_kernel,
        (
            jax.ShapeDtypeStruct((n, tokens, HEAD), BF),
            jax.ShapeDtypeStruct((n, HEAD + 16, tokens), BF),
        ),
        [ANY] * (2 * n),
        *all_k,
        *all_v,
        scratch_shapes=[pltpu.SemaphoreType.DMA((2, n))],
    )


def attend_kernel(
    shard_ids, first_q, second_q, kbuf, vbuf, first_out, second_out,
    qbuf, place, even, odd, acc, peak, tops, steps,
):
    n, tokens = kbuf.shape[0], kbuf.shape[1]
    tiles = ROWS // TILE
    side = TILE * HEADS
    big = 2 * side
    lane = iota((8, ROWS), 1)
    spots = []
    for c, query in enumerate((first_q, second_q)):
        meta = query[:, HEADS * HEAD :].astype(F32).T
        row_pos = meta[0:1, :] * 256.0 + meta[1:2, :]
        row_pos = jnp.where(meta[2:3, :] > 0.5, row_pos, -1.0)
        spots.append(row_pos)
        wide = jnp.broadcast_to(row_pos, (8, ROWS))
        for t in range(tiles):
            rows = slice(t * TILE, (t + 1) * TILE)
            spot = jnp.zeros((8, ROWS), F32)
            for h in range(HEADS):
                into = slice(c * side + h * TILE, c * side + (h + 1) * TILE)
                qbuf[t, into, :] = query[rows, h * HEAD : (h + 1) * HEAD]
                moved = pltpu.roll(wide, (h * TILE - t * TILE) % ROWS, 1)
                spot = jnp.where((lane >= h * TILE) & (lane < (h + 1) * TILE), moved, spot)
            place[t, :, c * side : (c + 1) * side] = spot.astype(jnp.int32)
    acc[...] = jnp.zeros_like(acc)
    peak[...] = jnp.full_like(peak, NEG)

    def below(limit):
        found = [jnp.sum(jnp.where(p < limit, 1.0, 0.0)).astype(jnp.int32) for p in spots]
        return jnp.minimum(*found), jnp.maximum(*found)

    bounds = []
    for i in range(n):
        start = (shard_ids[i] * tokens).astype(F32)
        bounds.append((below(start)[0], below(start + tokens)[1]))
    count = jnp.int32(0)
    clear = count
    for masked in (False, True):
        for i in range(n):
            least, most = bounds[i]
            for t in range(tiles):
                steps[count] = i * tiles + t
                cut = t * TILE < most
                here = (t >= least // TILE) & (cut if masked else ~cut)
                count += here.astype(jnp.int32)
        if not masked:
            clear = count
    for k in range(3):
        steps[count + k] = n * tiles

    def parts(code):
        none = code >= n * tiles
        i = jnp.where(none, 0, code // tiles)
        return i, jnp.where(none, 0, code % tiles), none

    span = 2 * HEAD

    def advance(made, into, made_top, used_step, source, top, masked):
        if made is not None:
            i, t, none = parts(made)
            start = jnp.where(none, 1 << 30, shard_ids[i] * tokens)
            rel = place[t] - start - iota((8, big), 0)
            best = jnp.full((8, big), -jnp.inf, F32)
        if used_step is not None:
            ui, ut, _ = parts(used_step)
            before = peak[ut][0:1, :]
            now = jnp.maximum(before, jnp.max(top[...], axis=0, keepdims=True))
            peak[ut] = jnp.broadcast_to(now, (8, big))
            summed = acc[ut] * jnp.exp(before - now)
        for k in range(tokens // span):
            at = slice(k * span, (k + 1) * span)
            if made is not None:
                s = lax.dot_general(
                    kbuf[i, at, :], qbuf[t], (((1,), (1,)), ((), ())), preferred_element_type=F32
                ).reshape(span // 8, 8, big)
                if masked:
                    keep = rel[None] >= 8 * iota((span // 8, 8, big), 0) + k * span
                    s = jnp.where(keep, s, -jnp.inf)
                best = jnp.maximum(best, jnp.max(s, axis=0))
                into[at, :] = s.reshape(span, big)
            if used_step is not None:
                weight = jnp.exp(source[at, :] - now).astype(BF)
                summed += jnp.dot(vbuf[ui, :, at], weight, preferred_element_type=F32)
        if used_step is not None:
            acc[ut] = summed
        if made is not None:
            made_top[...] = best

    def run(first, last, masked):
        def pair(j, _):
            a, b, c = steps[2 * j], steps[2 * j + 1], steps[2 * j + 2]
            advance(b, odd, tops.at[1], a, even, tops.at[0], masked)
            advance(c, even, tops.at[0], b, odd, tops.at[1], masked)
            return 0

        advance(steps[2 * first], even, tops.at[0], None, None, None, masked)
        lax.fori_loop(first, last, pair, 0)

    run(0, clear // 2, False)
    run(clear // 2, (count + 1) // 2, True)

    for c, out in enumerate((first_out, second_out)):
        lanes = slice(c * side, (c + 1) * side)
        for t in range(tiles):
            rows = slice(t * TILE, (t + 1) * TILE)
            numer = acc[t, :HEAD, lanes].T.astype(BF)
            pieces = three(peak[t, 0:1, lanes]) + three(acc[t, HEAD : HEAD + 1, lanes])
            block = jnp.zeros((META, side), F32)
            row = iota((META, side), 0)
            for k, piece in enumerate(pieces):
                block = jnp.where(row == k, piece, block)
            block = block.T
            stats = jnp.zeros((TILE, META), F32)
            for h in range(HEADS):
                out[rows, h * HEAD : (h + 1) * HEAD] = numer[h * TILE : (h + 1) * TILE, :]
                part = block[h * TILE : (h + 1) * TILE, :]
                stats += pltpu.roll(part, 8 * h, 1) if h else part
            out[rows, HEADS * HEAD :] = stats.astype(BF)


def attend(shard_ids, first_q, second_q, kbuf, vbuf):
    n, tokens = kbuf.shape[0], kbuf.shape[1]
    big = 2 * TILE * HEADS
    tiles = ROWS // TILE
    return call(
        attend_kernel,
        (jax.ShapeDtypeStruct((ROWS, HEADS * HEAD + META), BF),) * 2,
        [SM, VM, VM, VM, VM],
        shard_ids,
        first_q,
        second_q,
        kbuf,
        vbuf,
        flops=10**10,
        moved=7 * 10**6,
        scratch_shapes=[
            pltpu.VMEM((tiles, big, HEAD), BF),
            pltpu.VMEM((tiles, 8, big), jnp.int32),
            pltpu.VMEM((tokens, big), F32),
            pltpu.VMEM((tokens, big), F32),
            pltpu.VMEM((tiles, HEAD + 16, big), F32),
            pltpu.VMEM((tiles, 8, big), F32),
            pltpu.VMEM((2, 8, big), F32),
            pltpu.SMEM((n * tiles + 8,), jnp.int32),
        ],
    )


def output_kernel(weight, *refs):
    parts, out = refs[:-1], refs[-1]
    peaks, totals = [], []
    for part in parts:
        meta = part[:, HEADS * HEAD :].astype(F32)
        shifted = [meta] + [pltpu.roll(meta, META - c, 1) for c in range(1, 6)]
        peaks.append(shifted[0] + shifted[1] + shifted[2])
        totals.append(shifted[3] + shifted[4] + shifted[5])
    top = functools.reduce(jnp.maximum, peaks)
    fades = [jnp.exp(p - top) for p in peaks]
    denom = sum(f * t for f, t in zip(fades, totals))
    cols = []
    for h in range(HEADS):
        at = slice(h * HEAD, (h + 1) * HEAD)
        col = slice(8 * h, 8 * h + 1)
        numer = sum(f[:, col] * p[:, at].astype(F32) for f, p in zip(fades, parts))
        d = denom[:, col]
        cols.append((numer / jnp.where(d > 0.0, d, 1.0)).astype(BF))
    mixed = jnp.concatenate(cols, axis=1)
    width = out.shape[2]
    for z in range(out.shape[0]):
        out[z] = jnp.dot(
            mixed, weight[:, z * width : (z + 1) * width], preferred_element_type=F32
        ).astype(BF)


def spread_kernel(back, parts, out):
    total = parts[0].astype(F32)
    for z in range(1, parts.shape[0]):
        total += parts[z].astype(F32)
    out[...] = jnp.dot(back[...], total.astype(BF), preferred_element_type=F32).astype(BF)


def unpack_kernel(shards, count, got, out):
    s, count = seq_place(), count[0]
    slots, n = out.shape[0], got.shape[0]
    slot = iota((slots, n), 0)
    source = ((slot + s) & (shards - 1)) * GROUP + slot // shards
    pick = onehot((iota((slots, n), 1) == source) & (slot < count))
    out[...] = jnp.dot(pick, got[...], preferred_element_type=F32).astype(BF)


def shift(n, k):
    return [(i, (i + k) % n) for i in range(n)]


def body(hidden, norm_gain, w_query, w_out, keys, values, cand_count, cand_pos):
    x, y, c = (lax.axis_index(a) for a in SEQ)
    z = lax.axis_index("head")
    nx, ny, nc, nz = (lax.axis_size(a) for a in (*SEQ, "head"))
    shards = nx * ny * nc
    slots = cand_pos.shape[0]
    width = hidden.shape[1]
    lanes = shards * GROUP

    send = call(
        functools.partial(pack_kernel, shards),
        jax.ShapeDtypeStruct((lanes, width + META), BF),
        [SM, VM, VM],
        cand_count,
        cand_pos,
        hidden,
    )
    swap = [(0, 1), (1, 0)]
    keys, values, send = lax.optimization_barrier((keys, values, send))
    values = call(turn_kernel, jax.ShapeDtypeStruct(values.shape[::-1], BF), [VM], values)
    got = lax.all_to_all(send.reshape(shards, GROUP, -1), SEQ, 0, 0, tiled=True)
    got = got.reshape(lanes, -1)
    k_left, v_left = (
        lax.ppermute(a, SEQ[0], shift(nx, 1)) for a in (keys, values)
    )
    k_right, v_right = (
        lax.ppermute(a, SEQ[0], shift(nx, -1)) for a in (keys, values)
    )
    rows, meta, back = call(
        compact_kernel,
        (
            jax.ShapeDtypeStruct((ROWS, width), BF),
            jax.ShapeDtypeStruct((ROWS, META), BF),
            jax.ShapeDtypeStruct((lanes, ROWS), BF),
        ),
        [VM],
        got,
        flops=5 * 10**9,
        moved=10**6,
    )
    up, down = rows, rows
    slices, order = [rows], [0]
    for k in range(1, nz // 2 + 1):
        up = lax.ppermute(up, "head", shift(nz, 1))
        slices.append(up)
        order.append(-k)
        if k < nz // 2:
            down = lax.ppermute(down, "head", shift(nz, -1))
            slices.append(down)
            order.append(k)
            up, down = lax.optimization_barrier((up, down))

    k_far = lax.ppermute(k_left, SEQ[0], shift(nx, 1))
    v_far = lax.ppermute(v_right, SEQ[0], shift(nx, -1))
    near_k, near_v = [keys, k_left, k_right, k_far], [values, v_left, v_right, v_far]
    all_k = near_k + [lax.ppermute(a, SEQ[2], swap) for a in near_k[:3]]
    all_v = near_v + [lax.ppermute(a, SEQ[2], swap) for a in near_v[:3]]
    all_k.append(lax.ppermute(k_far, SEQ[2], swap))
    all_v.append(lax.ppermute(v_far, SEQ[2], swap))
    places = [((x + d) % nx, cc) for cc in (c, 1 - c) for d in (0, nx - 1, 1, 2)]
    shard_ids = jnp.stack([(px * ny + y) * nc + pc for px, pc in places]).astype(jnp.int32)

    half = HEAD // 2
    freq = jnp.exp(-math.log(ROPE_BASE) * 2.0 * jnp.arange(half, dtype=F32) / HEAD)
    meta_f = meta[:, :2].astype(F32)
    angle = (meta_f[:, 0:1] * 256.0 + meta_f[:, 1:2]) * freq[None, :]
    cosine, sine = jnp.cos(angle), jnp.sin(angle)
    cosine = jnp.concatenate([cosine, cosine], axis=1)
    sine = jnp.concatenate([-sine, sine], axis=1)

    w_query = pltpu.with_memory_space_constraint(w_query, pltpu.HBM)
    slices = [pltpu.with_memory_space_constraint(a, pltpu.HBM) for a in slices]
    query = call(
        functools.partial(project_kernel, tuple(order)),
        jax.ShapeDtypeStruct((ROWS, HEADS * HEAD + META), BF),
        [SM, VM, VM, VM, VM, HB] + [HB] * nz,
        z.reshape(1).astype(jnp.int32),
        meta,
        norm_gain.reshape(1, -1),
        cosine,
        sine,
        w_query,
        *slices,
        scratch_shapes=[
            pltpu.VMEM((nz, width, w_query.shape[1]), BF),
            pltpu.VMEM((nz, ROWS, width), BF),
            pltpu.SemaphoreType.DMA((nz,)),
            pltpu.SemaphoreType.DMA((nz,)),
        ],
    )

    asked = [(k, lax.ppermute(query, SEQ[1], shift(ny, k))) for k in (1, ny - 1, 2)]
    kbuf, vbuf = collect(all_k, all_v)
    (ka, qa), (kb, qb), (kc, qc) = asked
    own, ra = attend(shard_ids, query, qa, kbuf, vbuf)
    qb, qc, ra = lax.optimization_barrier((qb, qc, ra))
    ra = lax.ppermute(ra, SEQ[1], shift(ny, -ka))
    rb, rc = attend(shard_ids, qb, qc, kbuf, vbuf)
    parts = [own, ra]
    for k, r in ((kb, rb), (kc, rc)):
        parts.append(lax.ppermute(r, SEQ[1], shift(ny, -k)))

    partial = call(
        output_kernel,
        jax.ShapeDtypeStruct((nz, ROWS, width), BF),
        [VM] * (1 + ny),
        w_out,
        *parts,
    )
    arrived = lax.all_to_all(partial, "head", 0, 0, tiled=True)
    to_send = call(
        spread_kernel, jax.ShapeDtypeStruct((lanes, width), BF), [VM, VM], back, arrived
    )
    returned = lax.all_to_all(to_send.reshape(shards, GROUP, width), SEQ, 0, 0, tiled=True)
    return call(
        functools.partial(unpack_kernel, shards),
        jax.ShapeDtypeStruct((slots, width), BF),
        [SM, VM],
        cand_count,
        returned.reshape(lanes, width),
    )


def solution(mesh):
    split = Mesh(
        mesh.devices.reshape(4, 4, 2, mesh.shape["head"]), ("seq_0", "seq_1", "seq_2", "head")
    )
    placed = (
        P(SEQ, "head"),
        P(),
        P(None, "head"),
        P("head", None),
        P(SEQ, "head"),
        P(SEQ, "head"),
        P(SEQ),
        P(SEQ),
    )

    return jax.shard_map(
        body, mesh=split, in_specs=placed, out_specs=P(SEQ, "head"), check_vma=False
    )
```

```python
import functools
import math

import jax
import jax.numpy as jnp
from jax import lax
from jax.experimental import pallas as pl
from jax.experimental.pallas import tpu as pltpu
from jax.sharding import Mesh
from jax.sharding import PartitionSpec as P

HEAD = 128
HEADS = 4
ROWS = 128
GROUP = 16
META = 128
TILE = 32
SEQ = ("seq_0", "seq_1", "seq_2")
EPS = 1e-05
ROPE_BASE = 500000.0
NEG = -1e30
BF = jnp.bfloat16
F32 = jnp.float32
VM = pl.BlockSpec(memory_space=pltpu.VMEM)
SM = pl.BlockSpec(memory_space=pltpu.SMEM)
ANY = pl.BlockSpec(memory_space=pl.ANY)
HB = pl.BlockSpec(memory_space=pltpu.HBM)


def iota(shape, dim):
    return lax.broadcasted_iota(jnp.int32, shape, dim)


def onehot(mask):
    return jnp.where(mask, 1.0, 0.0).astype(BF)


def call(kernel, out, specs, *args, flops=0, moved=0, limit=20, **kw):
    return pl.pallas_call(
        kernel,
        out_shape=out,
        in_specs=specs,
        out_specs=jax.tree.map(lambda _: VM, out),
        cost_estimate=pl.CostEstimate(flops=flops, bytes_accessed=moved, transcendentals=0),
        compiler_params=pltpu.CompilerParams(vmem_limit_bytes=limit << 20),
        **kw,
    )(*args)


def seq_place():
    place = jnp.int32(0)
    for a in SEQ:
        place = place * lax.axis_size(a) + lax.axis_index(a)
    return place


def pack_kernel(shards, count, pos, hidden, out):
    s, count = seq_place(), count[0]
    slots, tokens, width = pos.shape[0], hidden.shape[0], hidden.shape[1]
    where = pos[...].reshape(1, slots)
    block = 128
    for b in range(shards * GROUP // block):
        o = iota((block, slots), 0) + b * block
        k = o & (GROUP - 1)
        slot = k * shards + (((o // GROUP) - s + shards) & (shards - 1))
        at = jnp.sum(
            jnp.where(iota((block, slots), 1) == slot, where, 0).astype(F32),
            axis=1,
            keepdims=True,
        ).astype(jnp.int32)
        oc = iota((block, 1), 0) + b * block
        kc = oc & (GROUP - 1)
        slot_c = kc * shards + (((oc // GROUP) - s + shards) & (shards - 1))
        live = (kc < slots // shards) & (slot_c < count)
        pick = onehot((iota((block, tokens), 1) == at) & live)
        rows = slice(b * block, (b + 1) * block)
        out[rows, :width] = jnp.dot(pick, hidden[...], preferred_element_type=F32).astype(BF)
        token = at + s * tokens
        lane = iota((block, META), 1)
        meta = jnp.where(lane == 0, token // 256, jnp.where(lane == 1, token & 255, 1))
        meta = jnp.where((lane < 3) & live, meta, 0)
        out[rows, width:] = meta.astype(F32).astype(BF)


def turn_kernel(values, out):
    out[...] = values[...].T


def compact_kernel(got, rows_out, meta_out, back_out):
    n = got.shape[0]
    width = got.shape[1] - META
    meta = got[:, width:]
    lower = onehot(iota((n, n), 0) >= iota((n, n), 1))
    running = jnp.dot(lower, meta, preferred_element_type=F32)[:, 2:3]
    live = meta.astype(F32)[:, 2:3]
    spare = ROWS - running[n - 1 : n, :]
    target = jnp.where(live > 0.5, running - 1.0 + spare, -1.0)
    back = jnp.where(iota((n, ROWS), 1).astype(F32) == target, 1.0, 0.0)
    back_out[...] = back.astype(BF)
    place = back.T.astype(BF)
    rows_out[...] = jnp.dot(place, got[:, :width], preferred_element_type=F32).astype(BF)
    meta_out[...] = jnp.dot(place, meta, preferred_element_type=F32).astype(BF)


def project_kernel(order, z, meta, gain, cosine, sine, weight, *refs):
    sources, (out, held, xs, sem, xsem) = refs[:-5], refs[-5:]
    width = xs.shape[2]
    n = len(sources)
    for k, x in enumerate(sources):
        pltpu.make_async_copy(x, xs.at[k], xsem.at[k]).start()
    spots = []
    for k, delta in enumerate(order):
        block = (z[0] + delta + n) & (n - 1)
        at = pl.ds(pl.multiple_of(block * width, width), width)
        pltpu.make_async_copy(weight.at[at], held.at[k], sem.at[k]).start()
        spots.append(at)
    total = jnp.zeros((ROWS, 1), F32)
    for k, x in enumerate(sources):
        pltpu.make_async_copy(x, xs.at[k], xsem.at[k]).wait()
        w = xs[k].astype(F32)
        total += jnp.sum(w * w, axis=1, keepdims=True)
    inv = lax.rsqrt(total / (n * width) + EPS)
    acc = jnp.zeros((ROWS, weight.shape[1]), F32)
    for k in range(n):
        normed = (xs[k].astype(F32) * inv * gain[:, spots[k]]).astype(BF)
        pltpu.make_async_copy(weight.at[spots[k]], held.at[k], sem.at[k]).wait()
        acc += jnp.dot(normed, held[k], preferred_element_type=F32)
    scale = 1.0 / math.sqrt(HEAD)
    for h in range(HEADS):
        at = slice(h * HEAD, (h + 1) * HEAD)
        part = acc[:, at]
        turned = part * cosine[...] + pltpu.roll(part, HEAD // 2, 1) * sine[...]
        out[:, at] = (turned * scale).astype(BF)
    out[:, HEADS * HEAD :] = meta[...]


def three(x):
    a = x.astype(BF).astype(F32)
    b = (x - a).astype(BF).astype(F32)
    return a, b, x - a - b


def collect_kernel(*refs):
    n = (len(refs) - 3) // 2
    keys, values = refs[:n], refs[n : 2 * n]
    kbuf, vbuf, sem = refs[2 * n :]
    copies = []
    for i in range(n):
        copies.append(pltpu.make_async_copy(keys[i], kbuf.at[i], sem.at[0, i]))
        copies.append(
            pltpu.make_async_copy(values[i], vbuf.at[i, pl.ds(0, HEAD)], sem.at[1, i])
        )
    for copy in copies:
        copy.start()
    vbuf[:, HEAD:, :] = jnp.ones((n, vbuf.shape[1] - HEAD, vbuf.shape[2]), BF)
    for copy in copies:
        copy.wait()


def collect(all_k, all_v):
    n = len(all_k)
    tokens = all_k[0].shape[0]
    return call(
        collect_kernel,
        (
            jax.ShapeDtypeStruct((n, tokens, HEAD), BF),
            jax.ShapeDtypeStruct((n, HEAD + 16, tokens), BF),
        ),
        [ANY] * (2 * n),
        *all_k,
        *all_v,
        scratch_shapes=[pltpu.SemaphoreType.DMA((2, n))],
    )


def attend_kernel(
    shard_ids, first_q, second_q, kbuf, vbuf, first_out, second_out,
    qbuf, place, even, odd, acc, peak, tops, steps,
):
    n, tokens = kbuf.shape[0], kbuf.shape[1]
    tiles = ROWS // TILE
    side = TILE * HEADS
    big = 2 * side
    lane = iota((8, ROWS), 1)
    spots = []
    for c, query in enumerate((first_q, second_q)):
        meta = query[:, HEADS * HEAD :].astype(F32).T
        row_pos = meta[0:1, :] * 256.0 + meta[1:2, :]
        row_pos = jnp.where(meta[2:3, :] > 0.5, row_pos, -1.0)
        spots.append(row_pos)
        wide = jnp.broadcast_to(row_pos, (8, ROWS))
        for t in range(tiles):
            rows = slice(t * TILE, (t + 1) * TILE)
            spot = jnp.zeros((8, ROWS), F32)
            for h in range(HEADS):
                into = slice(c * side + h * TILE, c * side + (h + 1) * TILE)
                qbuf[t, into, :] = query[rows, h * HEAD : (h + 1) * HEAD]
                moved = pltpu.roll(wide, (h * TILE - t * TILE) % ROWS, 1)
                spot = jnp.where((lane >= h * TILE) & (lane < (h + 1) * TILE), moved, spot)
            place[t, :, c * side : (c + 1) * side] = spot.astype(jnp.int32)
    acc[...] = jnp.zeros_like(acc)
    peak[...] = jnp.full_like(peak, NEG)

    def below(limit):
        found = [jnp.sum(jnp.where(p < limit, 1.0, 0.0)).astype(jnp.int32) for p in spots]
        return jnp.minimum(*found), jnp.maximum(*found)

    bounds = []
    for i in range(n):
        start = (shard_ids[i] * tokens).astype(F32)
        bounds.append((below(start)[0], below(start + tokens)[1]))
    count = jnp.int32(0)
    clear = count
    for masked in (False, True):
        for i in range(n):
            least, most = bounds[i]
            for t in range(tiles):
                steps[count] = i * tiles + t
                cut = t * TILE < most
                here = (t >= least // TILE) & (cut if masked else ~cut)
                count += here.astype(jnp.int32)
        if not masked:
            clear = count
    for k in range(3):
        steps[count + k] = n * tiles

    def parts(code):
        none = code >= n * tiles
        i = jnp.where(none, 0, code // tiles)
        return i, jnp.where(none, 0, code % tiles), none

    span = 2 * HEAD

    def advance(made, into, made_top, used_step, source, top, masked):
        if made is not None:
            i, t, none = parts(made)
            start = jnp.where(none, 1 << 30, shard_ids[i] * tokens)
            rel = place[t] - start - iota((8, big), 0)
            best = jnp.full((8, big), -jnp.inf, F32)
        if used_step is not None:
            ui, ut, _ = parts(used_step)
            before = peak[ut][0:1, :]
            now = jnp.maximum(before, jnp.max(top[...], axis=0, keepdims=True))
            peak[ut] = jnp.broadcast_to(now, (8, big))
            summed = acc[ut] * jnp.exp(before - now)
        for k in range(tokens // span):
            at = slice(k * span, (k + 1) * span)
            if made is not None:
                s = lax.dot_general(
                    kbuf[i, at, :], qbuf[t], (((1,), (1,)), ((), ())), preferred_element_type=F32
                ).reshape(span // 8, 8, big)
                if masked:
                    keep = rel[None] >= 8 * iota((span // 8, 8, big), 0) + k * span
                    s = jnp.where(keep, s, -jnp.inf)
                best = jnp.maximum(best, jnp.max(s, axis=0))
                into[at, :] = s.reshape(span, big)
            if used_step is not None:
                weight = jnp.exp(source[at, :] - now).astype(BF)
                summed += jnp.dot(vbuf[ui, :, at], weight, preferred_element_type=F32)
        if used_step is not None:
            acc[ut] = summed
        if made is not None:
            made_top[...] = best

    def run(first, last, masked):
        def pair(j, _):
            a, b, c = steps[2 * j], steps[2 * j + 1], steps[2 * j + 2]
            advance(b, odd, tops.at[1], a, even, tops.at[0], masked)
            advance(c, even, tops.at[0], b, odd, tops.at[1], masked)
            return 0

        advance(steps[2 * first], even, tops.at[0], None, None, None, masked)
        lax.fori_loop(first, last, pair, 0)

    run(0, clear // 2, False)
    run(clear // 2, (count + 1) // 2, True)

    for c, out in enumerate((first_out, second_out)):
        lanes = slice(c * side, (c + 1) * side)
        for t in range(tiles):
            rows = slice(t * TILE, (t + 1) * TILE)
            numer = acc[t, :HEAD, lanes].T.astype(BF)
            pieces = three(peak[t, 0:1, lanes]) + three(acc[t, HEAD : HEAD + 1, lanes])
            block = jnp.zeros((META, side), F32)
            row = iota((META, side), 0)
            for k, piece in enumerate(pieces):
                block = jnp.where(row == k, piece, block)
            block = block.T
            stats = jnp.zeros((TILE, META), F32)
            for h in range(HEADS):
                out[rows, h * HEAD : (h + 1) * HEAD] = numer[h * TILE : (h + 1) * TILE, :]
                part = block[h * TILE : (h + 1) * TILE, :]
                stats += pltpu.roll(part, 8 * h, 1) if h else part
            out[rows, HEADS * HEAD :] = stats.astype(BF)


def attend(shard_ids, first_q, second_q, kbuf, vbuf):
    n, tokens = kbuf.shape[0], kbuf.shape[1]
    big = 2 * TILE * HEADS
    tiles = ROWS // TILE
    return call(
        attend_kernel,
        (jax.ShapeDtypeStruct((ROWS, HEADS * HEAD + META), BF),) * 2,
        [SM, VM, VM, VM, VM],
        shard_ids,
        first_q,
        second_q,
        kbuf,
        vbuf,
        flops=10**10,
        moved=7 * 10**6,
        scratch_shapes=[
            pltpu.VMEM((tiles, big, HEAD), BF),
            pltpu.VMEM((tiles, 8, big), jnp.int32),
            pltpu.VMEM((tokens, big), F32),
            pltpu.VMEM((tokens, big), F32),
            pltpu.VMEM((tiles, HEAD + 16, big), F32),
            pltpu.VMEM((tiles, 8, big), F32),
            pltpu.VMEM((2, 8, big), F32),
            pltpu.SMEM((n * tiles + 8,), jnp.int32),
        ],
    )


def output_kernel(weight, *refs):
    parts, out = refs[:-1], refs[-1]
    peaks, totals = [], []
    for part in parts:
        meta = part[:, HEADS * HEAD :].astype(F32)
        shifted = [meta] + [pltpu.roll(meta, META - c, 1) for c in range(1, 6)]
        peaks.append(shifted[0] + shifted[1] + shifted[2])
        totals.append(shifted[3] + shifted[4] + shifted[5])
    top = functools.reduce(jnp.maximum, peaks)
    fades = [jnp.exp(p - top) for p in peaks]
    denom = sum(f * t for f, t in zip(fades, totals))
    cols = []
    for h in range(HEADS):
        at = slice(h * HEAD, (h + 1) * HEAD)
        col = slice(8 * h, 8 * h + 1)
        numer = sum(f[:, col] * p[:, at].astype(F32) for f, p in zip(fades, parts))
        d = denom[:, col]
        cols.append((numer / jnp.where(d > 0.0, d, 1.0)).astype(BF))
    mixed = jnp.concatenate(cols, axis=1)
    width = out.shape[2]
    for z in range(out.shape[0]):
        out[z] = jnp.dot(
            mixed, weight[:, z * width : (z + 1) * width], preferred_element_type=F32
        ).astype(BF)


def spread_kernel(back, parts, out):
    total = parts[0].astype(F32)
    for z in range(1, parts.shape[0]):
        total += parts[z].astype(F32)
    out[...] = jnp.dot(back[...], total.astype(BF), preferred_element_type=F32).astype(BF)


def unpack_kernel(shards, count, got, out):
    s, count = seq_place(), count[0]
    slots, n = out.shape[0], got.shape[0]
    slot = iota((slots, n), 0)
    source = ((slot + s) & (shards - 1)) * GROUP + slot // shards
    pick = onehot((iota((slots, n), 1) == source) & (slot < count))
    out[...] = jnp.dot(pick, got[...], preferred_element_type=F32).astype(BF)


def shift(n, k):
    return [(i, (i + k) % n) for i in range(n)]


def body(hidden, norm_gain, w_query, w_out, keys, values, cand_count, cand_pos):
    x, y, c = (lax.axis_index(a) for a in SEQ)
    z = lax.axis_index("head")
    nx, ny, nc, nz = (lax.axis_size(a) for a in (*SEQ, "head"))
    shards = nx * ny * nc
    slots = cand_pos.shape[0]
    width = hidden.shape[1]
    lanes = shards * GROUP

    send = call(
        functools.partial(pack_kernel, shards),
        jax.ShapeDtypeStruct((lanes, width + META), BF),
        [SM, VM, VM],
        cand_count,
        cand_pos,
        hidden,
    )
    swap = [(0, 1), (1, 0)]
    keys, values, send = lax.optimization_barrier((keys, values, send))
    values = call(turn_kernel, jax.ShapeDtypeStruct(values.shape[::-1], BF), [VM], values)
    got = lax.all_to_all(send.reshape(shards, GROUP, -1), SEQ, 0, 0, tiled=True)
    got = got.reshape(lanes, -1)
    k_left, v_left = (
        lax.ppermute(a, SEQ[0], shift(nx, 1)) for a in (keys, values)
    )
    k_right, v_right = (
        lax.ppermute(a, SEQ[0], shift(nx, -1)) for a in (keys, values)
    )
    rows, meta, back = call(
        compact_kernel,
        (
            jax.ShapeDtypeStruct((ROWS, width), BF),
            jax.ShapeDtypeStruct((ROWS, META), BF),
            jax.ShapeDtypeStruct((lanes, ROWS), BF),
        ),
        [VM],
        got,
        flops=5 * 10**9,
        moved=10**6,
    )
    up, down = rows, rows
    slices, order = [rows], [0]
    for k in range(1, nz // 2 + 1):
        up = lax.ppermute(up, "head", shift(nz, 1))
        slices.append(up)
        order.append(-k)
        if k < nz // 2:
            down = lax.ppermute(down, "head", shift(nz, -1))
            slices.append(down)
            order.append(k)
            up, down = lax.optimization_barrier((up, down))

    k_far = lax.ppermute(k_left, SEQ[0], shift(nx, 1))
    v_far = lax.ppermute(v_right, SEQ[0], shift(nx, -1))
    near_k, near_v = [keys, k_left, k_right, k_far], [values, v_left, v_right, v_far]
    all_k = near_k + [lax.ppermute(a, SEQ[2], swap) for a in near_k[:3]]
    all_v = near_v + [lax.ppermute(a, SEQ[2], swap) for a in near_v[:3]]
    all_k.append(lax.ppermute(k_far, SEQ[2], swap))
    all_v.append(lax.ppermute(v_far, SEQ[2], swap))
    places = [((x + d) % nx, cc) for cc in (c, 1 - c) for d in (0, nx - 1, 1, 2)]
    shard_ids = jnp.stack([(px * ny + y) * nc + pc for px, pc in places]).astype(jnp.int32)

    half = HEAD // 2
    freq = jnp.exp(-math.log(ROPE_BASE) * 2.0 * jnp.arange(half, dtype=F32) / HEAD)
    meta_f = meta[:, :2].astype(F32)
    angle = (meta_f[:, 0:1] * 256.0 + meta_f[:, 1:2]) * freq[None, :]
    cosine, sine = jnp.cos(angle), jnp.sin(angle)
    cosine = jnp.concatenate([cosine, cosine], axis=1)
    sine = jnp.concatenate([-sine, sine], axis=1)

    w_query = pltpu.with_memory_space_constraint(w_query, pltpu.HBM)
    slices = [pltpu.with_memory_space_constraint(a, pltpu.HBM) for a in slices]
    query = call(
        functools.partial(project_kernel, tuple(order)),
        jax.ShapeDtypeStruct((ROWS, HEADS * HEAD + META), BF),
        [SM, VM, VM, VM, VM, HB] + [HB] * nz,
        z.reshape(1).astype(jnp.int32),
        meta,
        norm_gain.reshape(1, -1),
        cosine,
        sine,
        w_query,
        *slices,
        scratch_shapes=[
            pltpu.VMEM((nz, width, w_query.shape[1]), BF),
            pltpu.VMEM((nz, ROWS, width), BF),
            pltpu.SemaphoreType.DMA((nz,)),
            pltpu.SemaphoreType.DMA((nz,)),
        ],
    )

    asked = [lax.ppermute(query, SEQ[1], shift(ny, k)) for k in (1, ny - 1)]
    far = lax.ppermute(query, SEQ[1], shift(ny, 2))
    kbuf, vbuf = collect(all_k, all_v)
    ra, rb = attend(shard_ids, *asked, kbuf, vbuf)
    query, far, ra, rb = lax.optimization_barrier((query, far, ra, rb))
    ra = lax.ppermute(ra, SEQ[1], shift(ny, -1))
    rb = lax.ppermute(rb, SEQ[1], shift(ny, 1))
    own, rc = attend(shard_ids, query, far, kbuf, vbuf)
    parts = [own, ra, rb, lax.ppermute(rc, SEQ[1], shift(ny, -2))]

    partial = call(
        output_kernel,
        jax.ShapeDtypeStruct((nz, ROWS, width), BF),
        [VM] * (1 + ny),
        w_out,
        *parts,
    )
    arrived = lax.all_to_all(partial, "head", 0, 0, tiled=True)
    to_send = call(
        spread_kernel, jax.ShapeDtypeStruct((lanes, width), BF), [VM, VM], back, arrived
    )
    returned = lax.all_to_all(to_send.reshape(shards, GROUP, width), SEQ, 0, 0, tiled=True)
    return call(
        functools.partial(unpack_kernel, shards),
        jax.ShapeDtypeStruct((slots, width), BF),
        [SM, VM],
        cand_count,
        returned.reshape(lanes, width),
    )


def solution(mesh):
    split = Mesh(
        mesh.devices.reshape(4, 4, 2, mesh.shape["head"]), ("seq_0", "seq_1", "seq_2", "head")
    )
    placed = (
        P(SEQ, "head"),
        P(),
        P(None, "head"),
        P("head", None),
        P(SEQ, "head"),
        P(SEQ, "head"),
        P(SEQ),
        P(SEQ),
    )

    return jax.shard_map(
        body, mesh=split, in_specs=placed, out_specs=P(SEQ, "head"), check_vma=False
    )
```

```python
import functools
import math

import jax
import jax.numpy as jnp
from jax import lax
from jax.experimental import pallas as pl
from jax.experimental.pallas import tpu as pltpu
from jax.sharding import Mesh
from jax.sharding import PartitionSpec as P

HEAD = 128
HEADS = 4
ROWS = 128
GROUP = 16
META = 128
TILE = 32
SEQ = ("seq_0", "seq_1", "seq_2")
EPS = 1e-05
ROPE_BASE = 500000.0
NEG = -1e30
BF = jnp.bfloat16
F32 = jnp.float32
VM = pl.BlockSpec(memory_space=pltpu.VMEM)
SM = pl.BlockSpec(memory_space=pltpu.SMEM)
ANY = pl.BlockSpec(memory_space=pl.ANY)
HB = pl.BlockSpec(memory_space=pltpu.HBM)


def iota(shape, dim):
    return lax.broadcasted_iota(jnp.int32, shape, dim)


def onehot(mask):
    return jnp.where(mask, 1.0, 0.0).astype(BF)


def call(kernel, out, specs, *args, flops=0, moved=0, limit=20, **kw):
    return pl.pallas_call(
        kernel,
        out_shape=out,
        in_specs=specs,
        out_specs=jax.tree.map(lambda _: VM, out),
        cost_estimate=pl.CostEstimate(flops=flops, bytes_accessed=moved, transcendentals=0),
        compiler_params=pltpu.CompilerParams(vmem_limit_bytes=limit << 20),
        **kw,
    )(*args)


def seq_place():
    place = jnp.int32(0)
    for a in SEQ:
        place = place * lax.axis_size(a) + lax.axis_index(a)
    return place


def pack_kernel(shards, count, pos, hidden, out):
    s, count = seq_place(), count[0]
    slots, tokens, width = pos.shape[0], hidden.shape[0], hidden.shape[1]
    where = pos[...].reshape(1, slots)
    block = 128
    for b in range(shards * GROUP // block):
        o = iota((block, slots), 0) + b * block
        k = o & (GROUP - 1)
        slot = k * shards + (((o // GROUP) - s + shards) & (shards - 1))
        at = jnp.sum(
            jnp.where(iota((block, slots), 1) == slot, where, 0).astype(F32),
            axis=1,
            keepdims=True,
        ).astype(jnp.int32)
        oc = iota((block, 1), 0) + b * block
        kc = oc & (GROUP - 1)
        slot_c = kc * shards + (((oc // GROUP) - s + shards) & (shards - 1))
        live = (kc < slots // shards) & (slot_c < count)
        pick = onehot((iota((block, tokens), 1) == at) & live)
        rows = slice(b * block, (b + 1) * block)
        out[rows, :width] = jnp.dot(pick, hidden[...], preferred_element_type=F32).astype(BF)
        token = at + s * tokens
        lane = iota((block, META), 1)
        meta = jnp.where(lane == 0, token // 256, jnp.where(lane == 1, token & 255, 1))
        meta = jnp.where((lane < 3) & live, meta, 0)
        out[rows, width:] = meta.astype(F32).astype(BF)


def turn_kernel(values, out):
    out[...] = values[...].T


def compact_kernel(got, rows_out, meta_out, back_out):
    n = got.shape[0]
    width = got.shape[1] - META
    meta = got[:, width:]
    lower = onehot(iota((n, n), 0) >= iota((n, n), 1))
    running = jnp.dot(lower, meta, preferred_element_type=F32)[:, 2:3]
    live = meta.astype(F32)[:, 2:3]
    spare = ROWS - running[n - 1 : n, :]
    target = jnp.where(live > 0.5, running - 1.0 + spare, -1.0)
    back = jnp.where(iota((n, ROWS), 1).astype(F32) == target, 1.0, 0.0)
    back_out[...] = back.astype(BF)
    place = back.T.astype(BF)
    rows_out[...] = jnp.dot(place, got[:, :width], preferred_element_type=F32).astype(BF)
    meta_out[...] = jnp.dot(place, meta, preferred_element_type=F32).astype(BF)


def project_kernel(order, z, meta, gain, cosine, sine, weight, *refs):
    sources, (out, held, xs, sem, xsem) = refs[:-5], refs[-5:]
    width = xs.shape[2]
    n = len(sources)
    for k, x in enumerate(sources):
        pltpu.make_async_copy(x, xs.at[k], xsem.at[k]).start()
    spots = []
    for k, delta in enumerate(order):
        block = (z[0] + delta + n) & (n - 1)
        at = pl.ds(pl.multiple_of(block * width, width), width)
        pltpu.make_async_copy(weight.at[at], held.at[k], sem.at[k]).start()
        spots.append(at)
    total = jnp.zeros((ROWS, 1), F32)
    for k, x in enumerate(sources):
        pltpu.make_async_copy(x, xs.at[k], xsem.at[k]).wait()
        w = xs[k].astype(F32)
        total += jnp.sum(w * w, axis=1, keepdims=True)
    inv = lax.rsqrt(total / (n * width) + EPS)
    acc = jnp.zeros((ROWS, weight.shape[1]), F32)
    for k in range(n):
        normed = (xs[k].astype(F32) * inv * gain[:, spots[k]]).astype(BF)
        pltpu.make_async_copy(weight.at[spots[k]], held.at[k], sem.at[k]).wait()
        acc += jnp.dot(normed, held[k], preferred_element_type=F32)
    scale = 1.0 / math.sqrt(HEAD)
    for h in range(HEADS):
        at = slice(h * HEAD, (h + 1) * HEAD)
        part = acc[:, at]
        turned = part * cosine[...] + pltpu.roll(part, HEAD // 2, 1) * sine[...]
        out[:, at] = (turned * scale).astype(BF)
    out[:, HEADS * HEAD :] = meta[...]


def three(x):
    a = x.astype(BF).astype(F32)
    b = (x - a).astype(BF).astype(F32)
    return a, b, x - a - b


def attend_kernel(n, shard_ids, first_q, second_q, *refs):
    loads = len(refs) > 2 * n
    keys, values = refs[:n], refs[n : 2 * n]
    if loads:
        first_out, second_out, kbuf, vbuf, *scratch, sem = refs[2 * n :]
        for i in range(n):
            pltpu.make_async_copy(keys[i], kbuf.at[i], sem.at[0, i]).start()
            pltpu.make_async_copy(values[i], vbuf.at[i, pl.ds(0, HEAD)], sem.at[1, i]).start()
        vbuf[:, HEAD:, :] = jnp.ones((n, vbuf.shape[1] - HEAD, vbuf.shape[2]), BF)
    else:
        kbuf, vbuf, first_out, second_out, *scratch = refs
    qbuf, place, even, odd, acc, peak, tops, steps = scratch
    tokens = kbuf.shape[1]
    tiles = ROWS // TILE
    side = TILE * HEADS
    big = 2 * side

    def arrive(done, *codes):
        if not loads:
            return done
        upto = done
        for code in codes:
            upto = jnp.maximum(upto, parts(code)[0] + 1)

        def wait(i, _):
            pltpu.make_async_copy(keys[0], kbuf.at[i], sem.at[0, i]).wait()
            pltpu.make_async_copy(values[0], vbuf.at[i, pl.ds(0, HEAD)], sem.at[1, i]).wait()
            return 0

        lax.fori_loop(done, upto, wait, 0)
        return upto

    lane = iota((8, ROWS), 1)
    spots = []
    for c, query in enumerate((first_q, second_q)):
        meta = query[:, HEADS * HEAD :].astype(F32).T
        row_pos = meta[0:1, :] * 256.0 + meta[1:2, :]
        row_pos = jnp.where(meta[2:3, :] > 0.5, row_pos, -1.0)
        spots.append(row_pos)
        wide = jnp.broadcast_to(row_pos, (8, ROWS))
        for t in range(tiles):
            rows = slice(t * TILE, (t + 1) * TILE)
            spot = jnp.zeros((8, ROWS), F32)
            for h in range(HEADS):
                into = slice(c * side + h * TILE, c * side + (h + 1) * TILE)
                qbuf[t, into, :] = query[rows, h * HEAD : (h + 1) * HEAD]
                moved = pltpu.roll(wide, (h * TILE - t * TILE) % ROWS, 1)
                spot = jnp.where((lane >= h * TILE) & (lane < (h + 1) * TILE), moved, spot)
            place[t, :, c * side : (c + 1) * side] = spot.astype(jnp.int32)
    acc[...] = jnp.zeros_like(acc)
    peak[...] = jnp.full_like(peak, NEG)

    def below(limit):
        found = [jnp.sum(jnp.where(p < limit, 1.0, 0.0)).astype(jnp.int32) for p in spots]
        return jnp.minimum(*found), jnp.maximum(*found)

    bounds = []
    for i in range(n):
        start = (shard_ids[i] * tokens).astype(F32)
        bounds.append((below(start)[0], below(start + tokens)[1]))
    count = jnp.int32(0)
    clear = count
    for masked in (False, True):
        for i in range(n):
            least, most = bounds[i]
            for t in range(tiles):
                steps[count] = i * tiles + t
                cut = t * TILE < most
                here = (t >= least // TILE) & (cut if masked else ~cut)
                count += here.astype(jnp.int32)
        if not masked:
            clear = count
    for k in range(3):
        steps[count + k] = n * tiles

    def parts(code):
        none = code >= n * tiles
        i = jnp.where(none, 0, code // tiles)
        return i, jnp.where(none, 0, code % tiles), none

    span = 2 * HEAD

    def advance(made, into, made_top, used_step, source, top, masked):
        if made is not None:
            i, t, none = parts(made)
            start = jnp.where(none, 1 << 30, shard_ids[i] * tokens)
            rel = place[t] - start - iota((8, big), 0)
            best = jnp.full((8, big), -jnp.inf, F32)
        if used_step is not None:
            ui, ut, _ = parts(used_step)
            before = peak[ut][0:1, :]
            now = jnp.maximum(before, jnp.max(top[...], axis=0, keepdims=True))
            peak[ut] = jnp.broadcast_to(now, (8, big))
            summed = acc[ut] * jnp.exp(before - now)
        for k in range(tokens // span):
            at = slice(k * span, (k + 1) * span)
            if made is not None:
                s = lax.dot_general(
                    kbuf[i, at, :], qbuf[t], (((1,), (1,)), ((), ())), preferred_element_type=F32
                ).reshape(span // 8, 8, big)
                if masked:
                    keep = rel[None] >= 8 * iota((span // 8, 8, big), 0) + k * span
                    s = jnp.where(keep, s, -jnp.inf)
                best = jnp.maximum(best, jnp.max(s, axis=0))
                into[at, :] = s.reshape(span, big)
            if used_step is not None:
                weight = jnp.exp(source[at, :] - now).astype(BF)
                summed += jnp.dot(vbuf[ui, :, at], weight, preferred_element_type=F32)
        if used_step is not None:
            acc[ut] = summed
        if made is not None:
            made_top[...] = best

    def run(done, first, last, masked):
        def pair(j, done):
            a, b, c = steps[2 * j], steps[2 * j + 1], steps[2 * j + 2]
            done = arrive(done, b, c)
            advance(b, odd, tops.at[1], a, even, tops.at[0], masked)
            advance(c, even, tops.at[0], b, odd, tops.at[1], masked)
            return done

        done = arrive(done, steps[2 * first])
        advance(steps[2 * first], even, tops.at[0], None, None, None, masked)
        return lax.fori_loop(first, last, pair, done)

    done = run(jnp.int32(0), 0, clear // 2, False)
    done = run(done, clear // 2, (count + 1) // 2, True)
    arrive(done, jnp.int32(n * tiles - 1))

    for c, out in enumerate((first_out, second_out)):
        lanes = slice(c * side, (c + 1) * side)
        for t in range(tiles):
            rows = slice(t * TILE, (t + 1) * TILE)
            numer = acc[t, :HEAD, lanes].T.astype(BF)
            pieces = three(peak[t, 0:1, lanes]) + three(acc[t, HEAD : HEAD + 1, lanes])
            block = jnp.zeros((META, side), F32)
            row = iota((META, side), 0)
            for k, piece in enumerate(pieces):
                block = jnp.where(row == k, piece, block)
            block = block.T
            stats = jnp.zeros((TILE, META), F32)
            for h in range(HEADS):
                out[rows, h * HEAD : (h + 1) * HEAD] = numer[h * TILE : (h + 1) * TILE, :]
                part = block[h * TILE : (h + 1) * TILE, :]
                stats += pltpu.roll(part, 8 * h, 1) if h else part
            out[rows, HEADS * HEAD :] = stats.astype(BF)


def attend(shard_ids, first_q, second_q, all_k, all_v):
    loads = isinstance(all_k, list)
    n = len(all_k) if loads else all_k.shape[0]
    tokens = all_k[0].shape[0]
    big = 2 * TILE * HEADS
    tiles = ROWS // TILE
    held = (
        jax.ShapeDtypeStruct((n, tokens, HEAD), BF),
        jax.ShapeDtypeStruct((n, HEAD + 16, tokens), BF),
    )
    sources = [*all_k, *all_v] if loads else [all_k, all_v]
    return call(
        functools.partial(attend_kernel, n),
        (jax.ShapeDtypeStruct((ROWS, HEADS * HEAD + META), BF),) * 2 + (held if loads else ()),
        [SM, VM, VM] + ([ANY] * (2 * n) if loads else [VM, VM]),
        shard_ids,
        first_q,
        second_q,
        *sources,
        flops=10**10,
        moved=7 * 10**6,
        scratch_shapes=[
            pltpu.VMEM((tiles, big, HEAD), BF),
            pltpu.VMEM((tiles, 8, big), jnp.int32),
            pltpu.VMEM((tokens, big), F32),
            pltpu.VMEM((tokens, big), F32),
            pltpu.VMEM((tiles, HEAD + 16, big), F32),
            pltpu.VMEM((tiles, 8, big), F32),
            pltpu.VMEM((2, 8, big), F32),
            pltpu.SMEM((n * tiles + 8,), jnp.int32),
        ]
        + ([pltpu.SemaphoreType.DMA((2, n))] if loads else []),
    )


def output_kernel(weight, *refs):
    parts, out = refs[:-1], refs[-1]
    peaks, totals = [], []
    for part in parts:
        meta = part[:, HEADS * HEAD :].astype(F32)
        shifted = [meta] + [pltpu.roll(meta, META - c, 1) for c in range(1, 6)]
        peaks.append(shifted[0] + shifted[1] + shifted[2])
        totals.append(shifted[3] + shifted[4] + shifted[5])
    top = functools.reduce(jnp.maximum, peaks)
    fades = [jnp.exp(p - top) for p in peaks]
    denom = sum(f * t for f, t in zip(fades, totals))
    cols = []
    for h in range(HEADS):
        at = slice(h * HEAD, (h + 1) * HEAD)
        col = slice(8 * h, 8 * h + 1)
        numer = sum(f[:, col] * p[:, at].astype(F32) for f, p in zip(fades, parts))
        d = denom[:, col]
        cols.append((numer / jnp.where(d > 0.0, d, 1.0)).astype(BF))
    mixed = jnp.concatenate(cols, axis=1)
    width = out.shape[2]
    for z in range(out.shape[0]):
        out[z] = jnp.dot(
            mixed, weight[:, z * width : (z + 1) * width], preferred_element_type=F32
        ).astype(BF)


def spread_kernel(back, parts, out):
    total = parts[0].astype(F32)
    for z in range(1, parts.shape[0]):
        total += parts[z].astype(F32)
    out[...] = jnp.dot(back[...], total.astype(BF), preferred_element_type=F32).astype(BF)


def unpack_kernel(shards, count, got, out):
    s, count = seq_place(), count[0]
    slots, n = out.shape[0], got.shape[0]
    slot = iota((slots, n), 0)
    source = ((slot + s) & (shards - 1)) * GROUP + slot // shards
    pick = onehot((iota((slots, n), 1) == source) & (slot < count))
    out[...] = jnp.dot(pick, got[...], preferred_element_type=F32).astype(BF)


def shift(n, k):
    return [(i, (i + k) % n) for i in range(n)]


def body(hidden, norm_gain, w_query, w_out, keys, values, cand_count, cand_pos):
    x, y, c = (lax.axis_index(a) for a in SEQ)
    z = lax.axis_index("head")
    nx, ny, nc, nz = (lax.axis_size(a) for a in (*SEQ, "head"))
    shards = nx * ny * nc
    slots = cand_pos.shape[0]
    width = hidden.shape[1]
    lanes = shards * GROUP

    send = call(
        functools.partial(pack_kernel, shards),
        jax.ShapeDtypeStruct((lanes, width + META), BF),
        [SM, VM, VM],
        cand_count,
        cand_pos,
        hidden,
    )
    swap = [(0, 1), (1, 0)]
    keys, values, send = lax.optimization_barrier((keys, values, send))
    values = call(turn_kernel, jax.ShapeDtypeStruct(values.shape[::-1], BF), [VM], values)
    got = lax.all_to_all(send.reshape(shards, GROUP, -1), SEQ, 0, 0, tiled=True)
    got = got.reshape(lanes, -1)
    k_left, v_left = (
        lax.ppermute(a, SEQ[0], shift(nx, 1)) for a in (keys, values)
    )
    k_right, v_right = (
        lax.ppermute(a, SEQ[0], shift(nx, -1)) for a in (keys, values)
    )
    rows, meta, back = call(
        compact_kernel,
        (
            jax.ShapeDtypeStruct((ROWS, width), BF),
            jax.ShapeDtypeStruct((ROWS, META), BF),
            jax.ShapeDtypeStruct((lanes, ROWS), BF),
        ),
        [VM],
        got,
        flops=5 * 10**9,
        moved=10**6,
    )
    up, down = rows, rows
    slices, order = [rows], [0]
    for k in range(1, nz // 2 + 1):
        up = lax.ppermute(up, "head", shift(nz, 1))
        slices.append(up)
        order.append(-k)
        if k < nz // 2:
            down = lax.ppermute(down, "head", shift(nz, -1))
            slices.append(down)
            order.append(k)
            up, down = lax.optimization_barrier((up, down))

    k_far = lax.ppermute(k_left, SEQ[0], shift(nx, 1))
    v_far = lax.ppermute(v_right, SEQ[0], shift(nx, -1))
    near_k, near_v = [keys, k_left, k_right, k_far], [values, v_left, v_right, v_far]
    all_k = near_k + [lax.ppermute(a, SEQ[2], swap) for a in near_k[:3]]
    all_v = near_v + [lax.ppermute(a, SEQ[2], swap) for a in near_v[:3]]
    all_k.append(lax.ppermute(k_far, SEQ[2], swap))
    all_v.append(lax.ppermute(v_far, SEQ[2], swap))
    places = [((x + d) % nx, cc) for cc in (c, 1 - c) for d in (0, nx - 1, 1, 2)]
    shard_ids = jnp.stack([(px * ny + y) * nc + pc for px, pc in places]).astype(jnp.int32)

    half = HEAD // 2
    freq = jnp.exp(-math.log(ROPE_BASE) * 2.0 * jnp.arange(half, dtype=F32) / HEAD)
    meta_f = meta[:, :2].astype(F32)
    angle = (meta_f[:, 0:1] * 256.0 + meta_f[:, 1:2]) * freq[None, :]
    cosine, sine = jnp.cos(angle), jnp.sin(angle)
    cosine = jnp.concatenate([cosine, cosine], axis=1)
    sine = jnp.concatenate([-sine, sine], axis=1)

    w_query = pltpu.with_memory_space_constraint(w_query, pltpu.HBM)
    slices[:-1] = [pltpu.with_memory_space_constraint(a, pltpu.HBM) for a in slices[:-1]]
    back = pltpu.with_memory_space_constraint(back, pltpu.HBM)
    query = call(
        functools.partial(project_kernel, tuple(order)),
        jax.ShapeDtypeStruct((ROWS, HEADS * HEAD + META), BF),
        [SM, VM, VM, VM, VM, HB] + [HB] * (nz - 1) + [ANY],
        z.reshape(1).astype(jnp.int32),
        meta,
        norm_gain.reshape(1, -1),
        cosine,
        sine,
        w_query,
        *slices,
        scratch_shapes=[
            pltpu.VMEM((nz, width, w_query.shape[1]), BF),
            pltpu.VMEM((nz, ROWS, width), BF),
            pltpu.SemaphoreType.DMA((nz,)),
            pltpu.SemaphoreType.DMA((nz,)),
        ],
    )

    asked = [lax.ppermute(query, SEQ[1], shift(ny, k)) for k in (1, ny - 1)]
    far = lax.ppermute(query, SEQ[1], shift(ny, 2))
    ra, rb, kbuf, vbuf = attend(shard_ids, *asked, all_k, all_v)
    query, far, ra, rb = lax.optimization_barrier((query, far, ra, rb))
    ra = lax.ppermute(ra, SEQ[1], shift(ny, -1))
    rb = lax.ppermute(rb, SEQ[1], shift(ny, 1))
    own, rc = attend(shard_ids, query, far, kbuf, vbuf)
    parts = [own, ra, rb, lax.ppermute(rc, SEQ[1], shift(ny, -2))]

    partial = call(
        output_kernel,
        jax.ShapeDtypeStruct((nz, ROWS, width), BF),
        [VM] * (1 + ny),
        w_out,
        *parts,
    )
    arrived = lax.all_to_all(partial, "head", 0, 0, tiled=True)
    to_send = call(
        spread_kernel, jax.ShapeDtypeStruct((lanes, width), BF), [VM, VM], back, arrived
    )
    returned = lax.all_to_all(to_send.reshape(shards, GROUP, width), SEQ, 0, 0, tiled=True)
    return call(
        functools.partial(unpack_kernel, shards),
        jax.ShapeDtypeStruct((slots, width), BF),
        [SM, VM],
        cand_count,
        returned.reshape(lanes, width),
    )


def solution(mesh):
    split = Mesh(
        mesh.devices.reshape(4, 4, 2, mesh.shape["head"]), ("seq_0", "seq_1", "seq_2", "head")
    )
    placed = (
        P(SEQ, "head"),
        P(),
        P(None, "head"),
        P("head", None),
        P(SEQ, "head"),
        P(SEQ, "head"),
        P(SEQ),
        P(SEQ),
    )

    return jax.shard_map(
        body, mesh=split, in_specs=placed, out_specs=P(SEQ, "head"), check_vma=False
    )
```

```python
import functools
import math

import jax
import jax.numpy as jnp
from jax import lax
from jax.experimental import pallas as pl
from jax.experimental.pallas import tpu as pltpu
from jax.sharding import Mesh
from jax.sharding import PartitionSpec as P

HEAD = 128
HEADS = 4
ROWS = 128
GROUP = 16
META = 128
TILE = 32
SEQ = ("seq_0", "seq_1", "seq_2")
EPS = 1e-05
ROPE_BASE = 500000.0
NEG = -1e30
BF = jnp.bfloat16
F32 = jnp.float32
VM = pl.BlockSpec(memory_space=pltpu.VMEM)
SM = pl.BlockSpec(memory_space=pltpu.SMEM)
ANY = pl.BlockSpec(memory_space=pl.ANY)
HB = pl.BlockSpec(memory_space=pltpu.HBM)


def iota(shape, dim):
    return lax.broadcasted_iota(jnp.int32, shape, dim)


def onehot(mask):
    return jnp.where(mask, 1.0, 0.0).astype(BF)


def call(kernel, out, specs, *args, flops=0, moved=0, limit=20, **kw):
    return pl.pallas_call(
        kernel,
        out_shape=out,
        in_specs=specs,
        out_specs=jax.tree.map(lambda _: VM, out),
        cost_estimate=pl.CostEstimate(flops=flops, bytes_accessed=moved, transcendentals=0),
        compiler_params=pltpu.CompilerParams(vmem_limit_bytes=limit << 20),
        **kw,
    )(*args)


def seq_place():
    place = jnp.int32(0)
    for a in SEQ:
        place = place * lax.axis_size(a) + lax.axis_index(a)
    return place


def pack_kernel(shards, count, pos_from, hidden_from, out, pos, hidden, sem):
    load_pos = pltpu.make_async_copy(pos_from, pos, sem.at[0])
    load_rows = pltpu.make_async_copy(hidden_from, hidden, sem.at[1])
    load_pos.start()
    load_rows.start()
    s, count = seq_place(), count[0]
    slots, tokens, width = pos.shape[0], hidden.shape[0], hidden.shape[1]
    load_pos.wait()
    where = pos[...].reshape(1, slots)
    block = 128
    for b in range(shards * GROUP // block):
        o = iota((block, slots), 0) + b * block
        k = o & (GROUP - 1)
        slot = k * shards + (((o // GROUP) - s + shards) & (shards - 1))
        at = jnp.sum(
            jnp.where(iota((block, slots), 1) == slot, where, 0).astype(F32),
            axis=1,
            keepdims=True,
        ).astype(jnp.int32)
        oc = iota((block, 1), 0) + b * block
        kc = oc & (GROUP - 1)
        slot_c = kc * shards + (((oc // GROUP) - s + shards) & (shards - 1))
        live = (kc < slots // shards) & (slot_c < count)
        pick = onehot((iota((block, tokens), 1) == at) & live)
        rows = slice(b * block, (b + 1) * block)
        if b == 0:
            load_rows.wait()
        out[rows, :width] = jnp.dot(pick, hidden[...], preferred_element_type=F32).astype(BF)
        token = at + s * tokens
        lane = iota((block, META), 1)
        meta = jnp.where(lane == 0, token // 256, jnp.where(lane == 1, token & 255, 1))
        meta = jnp.where((lane < 3) & live, meta, 0)
        out[rows, width:] = meta.astype(F32).astype(BF)


def turn_kernel(values, out):
    out[...] = values[...].T


def compact_kernel(got, rows_out, meta_out, back_out):
    n = got.shape[0]
    width = got.shape[1] - META
    meta = got[:, width:]
    lower = onehot(iota((n, n), 0) >= iota((n, n), 1))
    running = jnp.dot(lower, meta, preferred_element_type=F32)[:, 2:3]
    live = meta.astype(F32)[:, 2:3]
    spare = ROWS - running[n - 1 : n, :]
    target = jnp.where(live > 0.5, running - 1.0 + spare, -1.0)
    back = jnp.where(iota((n, ROWS), 1).astype(F32) == target, 1.0, 0.0)
    back_out[...] = back.astype(BF)
    place = back.T.astype(BF)
    rows_out[...] = jnp.dot(place, got[:, :width], preferred_element_type=F32).astype(BF)
    meta_out[...] = jnp.dot(place, meta, preferred_element_type=F32).astype(BF)


def project_kernel(order, z, meta, gain, cosine, sine, weight, *refs):
    sources, (out, held, xs, sem, xsem) = refs[:-5], refs[-5:]
    width = xs.shape[2]
    n = len(sources)
    for k, x in enumerate(sources):
        pltpu.make_async_copy(x, xs.at[k], xsem.at[k]).start()
    spots = []
    for k, delta in enumerate(order):
        block = (z[0] + delta + n) & (n - 1)
        at = pl.ds(pl.multiple_of(block * width, width), width)
        pltpu.make_async_copy(weight.at[at], held.at[k], sem.at[k]).start()
        spots.append(at)
    total = jnp.zeros((ROWS, 1), F32)
    for k, x in enumerate(sources):
        pltpu.make_async_copy(x, xs.at[k], xsem.at[k]).wait()
        w = xs[k].astype(F32)
        total += jnp.sum(w * w, axis=1, keepdims=True)
    inv = lax.rsqrt(total / (n * width) + EPS)
    acc = jnp.zeros((ROWS, weight.shape[1]), F32)
    for k in range(n):
        normed = (xs[k].astype(F32) * inv * gain[:, spots[k]]).astype(BF)
        pltpu.make_async_copy(weight.at[spots[k]], held.at[k], sem.at[k]).wait()
        acc += jnp.dot(normed, held[k], preferred_element_type=F32)
    scale = 1.0 / math.sqrt(HEAD)
    for h in range(HEADS):
        at = slice(h * HEAD, (h + 1) * HEAD)
        part = acc[:, at]
        turned = part * cosine[...] + pltpu.roll(part, HEAD // 2, 1) * sine[...]
        out[:, at] = (turned * scale).astype(BF)
    out[:, HEADS * HEAD :] = meta[...]


def three(x):
    a = x.astype(BF).astype(F32)
    b = (x - a).astype(BF).astype(F32)
    return a, b, x - a - b


def attend_kernel(n, shard_ids, first_q, second_q, *refs):
    loads = len(refs) > 2 * n
    keys, values = refs[:n], refs[n : 2 * n]
    if loads:
        first_out, second_out, kbuf, vbuf, *scratch, sem = refs[2 * n :]
        for i in range(n):
            pltpu.make_async_copy(keys[i], kbuf.at[i], sem.at[0, i]).start()
            pltpu.make_async_copy(values[i], vbuf.at[i, pl.ds(0, HEAD)], sem.at[1, i]).start()
        vbuf[:, HEAD:, :] = jnp.ones((n, vbuf.shape[1] - HEAD, vbuf.shape[2]), BF)
    else:
        kbuf, vbuf, first_out, second_out, *scratch = refs
    qbuf, place, even, odd, acc, peak, tops, steps = scratch
    tokens = kbuf.shape[1]
    tiles = ROWS // TILE
    side = TILE * HEADS
    big = 2 * side

    def arrive(done, *codes):
        if not loads:
            return done
        upto = done
        for code in codes:
            upto = jnp.maximum(upto, parts(code)[0] + 1)

        def wait(i, _):
            pltpu.make_async_copy(keys[0], kbuf.at[i], sem.at[0, i]).wait()
            pltpu.make_async_copy(values[0], vbuf.at[i, pl.ds(0, HEAD)], sem.at[1, i]).wait()
            return 0

        lax.fori_loop(done, upto, wait, 0)
        return upto

    lane = iota((8, ROWS), 1)
    spots = []
    for c, query in enumerate((first_q, second_q)):
        meta = query[:, HEADS * HEAD :].astype(F32).T
        row_pos = meta[0:1, :] * 256.0 + meta[1:2, :]
        row_pos = jnp.where(meta[2:3, :] > 0.5, row_pos, -1.0)
        spots.append(row_pos)
        wide = jnp.broadcast_to(row_pos, (8, ROWS))
        for t in range(tiles):
            rows = slice(t * TILE, (t + 1) * TILE)
            spot = jnp.zeros((8, ROWS), F32)
            for h in range(HEADS):
                into = slice(c * side + h * TILE, c * side + (h + 1) * TILE)
                qbuf[t, into, :] = query[rows, h * HEAD : (h + 1) * HEAD]
                moved = pltpu.roll(wide, (h * TILE - t * TILE) % ROWS, 1)
                spot = jnp.where((lane >= h * TILE) & (lane < (h + 1) * TILE), moved, spot)
            place[t, :, c * side : (c + 1) * side] = spot.astype(jnp.int32)
    acc[...] = jnp.zeros_like(acc)
    peak[...] = jnp.full_like(peak, NEG)

    def below(limit):
        found = [jnp.sum(jnp.where(p < limit, 1.0, 0.0)).astype(jnp.int32) for p in spots]
        return jnp.minimum(*found), jnp.maximum(*found)

    bounds = []
    for i in range(n):
        start = (shard_ids[i] * tokens).astype(F32)
        bounds.append((below(start)[0], below(start + tokens)[1]))
    count = jnp.int32(1)
    cut_off = count
    steps[0] = n * tiles
    for masked in (True, False):
        for i in range(n):
            least, most = bounds[i]
            for t in range(tiles):
                steps[count] = i * tiles + t
                cut = t * TILE < most
                here = (t >= least // TILE) & (cut if masked else ~cut)
                count += here.astype(jnp.int32)
        if masked:
            cut_off = count
    for k in range(3):
        steps[count + k] = n * tiles
    base = count & 1
    middle = (cut_off - base + 1) // 2

    def parts(code):
        none = code >= n * tiles
        i = jnp.where(none, 0, code // tiles)
        return i, jnp.where(none, 0, code % tiles), none

    span = 2 * HEAD

    def advance(made, into, made_top, used_step, source, top, masked):
        if made is not None:
            i, t, none = parts(made)
            start = jnp.where(none, 1 << 30, shard_ids[i] * tokens)
            rel = place[t] - start - iota((8, big), 0)
            best = jnp.full((8, big), -jnp.inf, F32)
        if used_step is not None:
            ui, ut, _ = parts(used_step)
            before = peak[ut][0:1, :]
            now = jnp.maximum(before, jnp.max(top[...], axis=0, keepdims=True))
            peak[ut] = jnp.broadcast_to(now, (8, big))
            summed = acc[ut] * jnp.exp(before - now)
        for k in range(tokens // span):
            at = slice(k * span, (k + 1) * span)
            if made is not None:
                s = lax.dot_general(
                    kbuf[i, at, :], qbuf[t], (((1,), (1,)), ((), ())), preferred_element_type=F32
                ).reshape(span // 8, 8, big)
                if masked:
                    keep = rel[None] >= 8 * iota((span // 8, 8, big), 0) + k * span
                    s = jnp.where(keep, s, -jnp.inf)
                best = jnp.maximum(best, jnp.max(s, axis=0))
                into[at, :] = s.reshape(span, big)
            if used_step is not None:
                weight = jnp.exp(source[at, :] - now).astype(BF)
                summed += jnp.dot(vbuf[ui, :, at], weight, preferred_element_type=F32)
        if used_step is not None:
            acc[ut] = summed
        if made is not None:
            made_top[...] = best

    def run(done, first, last, masked):
        def pair(j, done):
            a, b, c = steps[base + 2 * j], steps[base + 2 * j + 1], steps[base + 2 * j + 2]
            done = arrive(done, b, c)
            advance(b, odd, tops.at[1], a, even, tops.at[0], masked)
            advance(c, even, tops.at[0], b, odd, tops.at[1], masked)
            return done

        done = arrive(done, steps[base + 2 * first])
        advance(steps[base + 2 * first], even, tops.at[0], None, None, None, masked)
        return lax.fori_loop(first, last, pair, done)

    done = run(jnp.int32(0), 0, middle, True)
    done = run(done, middle, (count - base) // 2, False)
    arrive(done, jnp.int32(n * tiles - 1))

    for c, out in enumerate((first_out, second_out)):
        lanes = slice(c * side, (c + 1) * side)
        for t in range(tiles):
            rows = slice(t * TILE, (t + 1) * TILE)
            numer = acc[t, :HEAD, lanes].T.astype(BF)
            pieces = three(peak[t, 0:1, lanes]) + three(acc[t, HEAD : HEAD + 1, lanes])
            block = jnp.zeros((META, side), F32)
            row = iota((META, side), 0)
            for k, piece in enumerate(pieces):
                block = jnp.where(row == k, piece, block)
            block = block.T
            stats = jnp.zeros((TILE, META), F32)
            for h in range(HEADS):
                out[rows, h * HEAD : (h + 1) * HEAD] = numer[h * TILE : (h + 1) * TILE, :]
                part = block[h * TILE : (h + 1) * TILE, :]
                stats += pltpu.roll(part, 8 * h, 1) if h else part
            out[rows, HEADS * HEAD :] = stats.astype(BF)


def attend(shard_ids, first_q, second_q, all_k, all_v):
    loads = isinstance(all_k, list)
    n = len(all_k) if loads else all_k.shape[0]
    tokens = all_k[0].shape[0]
    big = 2 * TILE * HEADS
    tiles = ROWS // TILE
    held = (
        jax.ShapeDtypeStruct((n, tokens, HEAD), BF),
        jax.ShapeDtypeStruct((n, HEAD + 16, tokens), BF),
    )
    sources = [*all_k, *all_v] if loads else [all_k, all_v]
    return call(
        functools.partial(attend_kernel, n),
        (jax.ShapeDtypeStruct((ROWS, HEADS * HEAD + META), BF),) * 2 + (held if loads else ()),
        [SM, VM, VM] + ([ANY] * (2 * n) if loads else [VM, VM]),
        shard_ids,
        first_q,
        second_q,
        *sources,
        flops=10**10,
        moved=7 * 10**6,
        scratch_shapes=[
            pltpu.VMEM((tiles, big, HEAD), BF),
            pltpu.VMEM((tiles, 8, big), jnp.int32),
            pltpu.VMEM((tokens, big), F32),
            pltpu.VMEM((tokens, big), F32),
            pltpu.VMEM((tiles, HEAD + 16, big), F32),
            pltpu.VMEM((tiles, 8, big), F32),
            pltpu.VMEM((2, 8, big), F32),
            pltpu.SMEM((n * tiles + 8,), jnp.int32),
        ]
        + ([pltpu.SemaphoreType.DMA((2, n))] if loads else []),
    )


def output_kernel(weight, *refs):
    parts, out = refs[:-1], refs[-1]
    peaks, totals = [], []
    for part in parts:
        meta = part[:, HEADS * HEAD :].astype(F32)
        shifted = [meta] + [pltpu.roll(meta, META - c, 1) for c in range(1, 6)]
        peaks.append(shifted[0] + shifted[1] + shifted[2])
        totals.append(shifted[3] + shifted[4] + shifted[5])
    top = functools.reduce(jnp.maximum, peaks)
    fades = [jnp.exp(p - top) for p in peaks]
    denom = sum(f * t for f, t in zip(fades, totals))
    cols = []
    for h in range(HEADS):
        at = slice(h * HEAD, (h + 1) * HEAD)
        col = slice(8 * h, 8 * h + 1)
        numer = sum(f[:, col] * p[:, at].astype(F32) for f, p in zip(fades, parts))
        d = denom[:, col]
        cols.append((numer / jnp.where(d > 0.0, d, 1.0)).astype(BF))
    mixed = jnp.concatenate(cols, axis=1)
    width = out.shape[2]
    for z in range(out.shape[0]):
        out[z] = jnp.dot(
            mixed, weight[:, z * width : (z + 1) * width], preferred_element_type=F32
        ).astype(BF)


def spread_kernel(back, parts, out):
    total = parts[0].astype(F32)
    for z in range(1, parts.shape[0]):
        total += parts[z].astype(F32)
    out[...] = jnp.dot(back[...], total.astype(BF), preferred_element_type=F32).astype(BF)


def unpack_kernel(shards, count, got, out):
    s, count = seq_place(), count[0]
    slots, n = out.shape[0], got.shape[0]
    slot = iota((slots, n), 0)
    source = ((slot + s) & (shards - 1)) * GROUP + slot // shards
    pick = onehot((iota((slots, n), 1) == source) & (slot < count))
    out[...] = jnp.dot(pick, got[...], preferred_element_type=F32).astype(BF)


def shift(n, k):
    return [(i, (i + k) % n) for i in range(n)]


def body(hidden, norm_gain, w_query, w_out, keys, values, cand_count, cand_pos):
    x, y, c = (lax.axis_index(a) for a in SEQ)
    z = lax.axis_index("head")
    nx, ny, nc, nz = (lax.axis_size(a) for a in (*SEQ, "head"))
    shards = nx * ny * nc
    slots = cand_pos.shape[0]
    width = hidden.shape[1]
    lanes = shards * GROUP

    send = call(
        functools.partial(pack_kernel, shards),
        jax.ShapeDtypeStruct((lanes, width + META), BF),
        [SM, HB, HB],
        cand_count,
        pltpu.with_memory_space_constraint(cand_pos, pltpu.HBM),
        pltpu.with_memory_space_constraint(hidden, pltpu.HBM),
        scratch_shapes=[
            pltpu.VMEM(cand_pos.shape, jnp.int32),
            pltpu.VMEM(hidden.shape, BF),
            pltpu.SemaphoreType.DMA((2,)),
        ],
    )
    swap = [(0, 1), (1, 0)]
    keys, values, send = lax.optimization_barrier((keys, values, send))
    values = call(turn_kernel, jax.ShapeDtypeStruct(values.shape[::-1], BF), [VM], values)
    got = lax.all_to_all(send.reshape(shards, GROUP, -1), SEQ, 0, 0, tiled=True)
    got = got.reshape(lanes, -1)
    plane = SEQ[:2]

    def mirrored(row, col):
        return col if row % 2 == 0 else ny - 1 - col

    def move(a, step):
        pairs = [
            (r * ny + q, (r + step) % nx * ny + mirrored(r, q)) for r in range(nx) for q in range(ny)
        ]
        return lax.ppermute(a, plane, pairs)

    k_left, k_right = move(keys, 1), move(keys, -1)
    v_left, v_right = move(values, 1), move(values, -1)
    k_own, v_own = move(keys, 0), move(values, 0)
    rows, meta, back = call(
        compact_kernel,
        (
            jax.ShapeDtypeStruct((ROWS, width), BF),
            jax.ShapeDtypeStruct((ROWS, META), BF),
            jax.ShapeDtypeStruct((lanes, ROWS), BF),
        ),
        [VM],
        got,
        flops=5 * 10**9,
        moved=10**6,
    )
    up, down = rows, rows
    slices, order = [rows], [0]
    for k in range(1, nz // 2 + 1):
        up = lax.ppermute(up, "head", shift(nz, 1))
        slices.append(up)
        order.append(-k)
        if k < nz // 2:
            down = lax.ppermute(down, "head", shift(nz, -1))
            slices.append(down)
            order.append(k)
            up, down = lax.optimization_barrier((up, down))

    k_far = lax.ppermute(k_left, SEQ[0], shift(nx, 1))
    v_far = lax.ppermute(v_right, SEQ[0], shift(nx, -1))
    near_k, near_v = [k_own, k_left, k_right, k_far], [v_own, v_left, v_right, v_far]
    all_k = near_k + [lax.ppermute(a, SEQ[2], swap) for a in near_k[:3]]
    all_v = near_v + [lax.ppermute(a, SEQ[2], swap) for a in near_v[:3]]
    all_k.append(lax.ppermute(k_far, SEQ[2], swap))
    all_v.append(lax.ppermute(v_far, SEQ[2], swap))
    places = [((x + d) % nx, cc) for cc in (c, 1 - c) for d in (0, nx - 1, 1, 2)]
    shard_ids = jnp.stack(
        [(px * ny + jnp.where(px % 2 == 0, y, ny - 1 - y)) * nc + pc for px, pc in places]
    ).astype(jnp.int32)

    half = HEAD // 2
    freq = jnp.exp(-math.log(ROPE_BASE) * 2.0 * jnp.arange(half, dtype=F32) / HEAD)
    meta_f = meta[:, :2].astype(F32)
    angle = (meta_f[:, 0:1] * 256.0 + meta_f[:, 1:2]) * freq[None, :]
    cosine, sine = jnp.cos(angle), jnp.sin(angle)
    cosine = jnp.concatenate([cosine, cosine], axis=1)
    sine = jnp.concatenate([-sine, sine], axis=1)

    w_query = pltpu.with_memory_space_constraint(w_query, pltpu.HBM)
    slices[:-1] = [pltpu.with_memory_space_constraint(a, pltpu.HBM) for a in slices[:-1]]
    back = pltpu.with_memory_space_constraint(back, pltpu.HBM)
    query = call(
        functools.partial(project_kernel, tuple(order)),
        jax.ShapeDtypeStruct((ROWS, HEADS * HEAD + META), BF),
        [SM, VM, VM, VM, VM, HB] + [HB] * (nz - 1) + [ANY],
        z.reshape(1).astype(jnp.int32),
        meta,
        norm_gain.reshape(1, -1),
        cosine,
        sine,
        w_query,
        *slices,
        scratch_shapes=[
            pltpu.VMEM((nz, width, w_query.shape[1]), BF),
            pltpu.VMEM((nz, ROWS, width), BF),
            pltpu.SemaphoreType.DMA((nz,)),
            pltpu.SemaphoreType.DMA((nz,)),
        ],
    )

    asked = [lax.ppermute(query, SEQ[1], shift(ny, k)) for k in (1, ny - 1)]
    far = lax.ppermute(query, SEQ[1], shift(ny, 2))
    ra, rb, kbuf, vbuf = attend(shard_ids, *asked, all_k, all_v)
    query, far, ra, rb = lax.optimization_barrier((query, far, ra, rb))
    ra = lax.ppermute(ra, SEQ[1], shift(ny, -1))
    rb = lax.ppermute(rb, SEQ[1], shift(ny, 1))
    own, rc = attend(shard_ids, query, far, kbuf, vbuf)
    parts = [own, ra, rb, lax.ppermute(rc, SEQ[1], shift(ny, -2))]

    partial = call(
        output_kernel,
        jax.ShapeDtypeStruct((nz, ROWS, width), BF),
        [VM] * (1 + ny),
        w_out,
        *parts,
    )
    arrived = lax.all_to_all(partial, "head", 0, 0, tiled=True)
    to_send = call(
        spread_kernel, jax.ShapeDtypeStruct((lanes, width), BF), [VM, VM], back, arrived
    )
    returned = lax.all_to_all(to_send.reshape(shards, GROUP, width), SEQ, 0, 0, tiled=True)
    return call(
        functools.partial(unpack_kernel, shards),
        jax.ShapeDtypeStruct((slots, width), BF),
        [SM, VM],
        cand_count,
        returned.reshape(lanes, width),
    )


def solution(mesh):
    split = Mesh(
        mesh.devices.reshape(4, 4, 2, mesh.shape["head"]), ("seq_0", "seq_1", "seq_2", "head")
    )
    placed = (
        P(SEQ, "head"),
        P(),
        P(None, "head"),
        P("head", None),
        P(SEQ, "head"),
        P(SEQ, "head"),
        P(SEQ),
        P(SEQ),
    )

    return jax.shard_map(
        body, mesh=split, in_specs=placed, out_specs=P(SEQ, "head"), check_vma=False
    )
```

```python
import functools
import math

import jax
import jax.numpy as jnp
from jax import lax
from jax.experimental import pallas as pl
from jax.experimental.pallas import tpu as pltpu
from jax.sharding import Mesh
from jax.sharding import PartitionSpec as P

HEAD = 128
HEADS = 4
ROWS = 128
GROUP = 16
META = 128
TILE = 32
SEQ = ("seq_0", "seq_1", "seq_2")
EPS = 1e-05
ROPE_BASE = 500000.0
NEG = -1e30
BF = jnp.bfloat16
F32 = jnp.float32
VM = pl.BlockSpec(memory_space=pltpu.VMEM)
SM = pl.BlockSpec(memory_space=pltpu.SMEM)
ANY = pl.BlockSpec(memory_space=pl.ANY)
HB = pl.BlockSpec(memory_space=pltpu.HBM)


def iota(shape, dim):
    return lax.broadcasted_iota(jnp.int32, shape, dim)


def onehot(mask):
    return jnp.where(mask, 1.0, 0.0).astype(BF)


def call(kernel, out, specs, *args, flops=0, moved=0, limit=20, **kw):
    return pl.pallas_call(
        kernel,
        out_shape=out,
        in_specs=specs,
        out_specs=jax.tree.map(lambda _: VM, out),
        cost_estimate=pl.CostEstimate(flops=flops, bytes_accessed=moved, transcendentals=0),
        compiler_params=pltpu.CompilerParams(vmem_limit_bytes=limit << 20),
        **kw,
    )(*args)


def seq_place():
    place = jnp.int32(0)
    for a in SEQ:
        place = place * lax.axis_size(a) + lax.axis_index(a)
    return place


def pack_kernel(shards, count, pos, hidden, out):
    s, count = seq_place(), count[0]
    slots, tokens, width = pos.shape[0], hidden.shape[0], hidden.shape[1]
    where = pos[...].reshape(1, slots)
    block = 128
    for b in range(shards * GROUP // block):
        o = iota((block, slots), 0) + b * block
        k = o & (GROUP - 1)
        slot = k * shards + (((o // GROUP) - s + shards) & (shards - 1))
        at = jnp.sum(
            jnp.where(iota((block, slots), 1) == slot, where, 0).astype(F32),
            axis=1,
            keepdims=True,
        ).astype(jnp.int32)
        oc = iota((block, 1), 0) + b * block
        kc = oc & (GROUP - 1)
        slot_c = kc * shards + (((oc // GROUP) - s + shards) & (shards - 1))
        live = (kc < slots // shards) & (slot_c < count)
        pick = onehot((iota((block, tokens), 1) == at) & live)
        rows = slice(b * block, (b + 1) * block)
        out[rows, :width] = jnp.dot(pick, hidden[...], preferred_element_type=F32).astype(BF)
        token = at + s * tokens
        lane = iota((block, META), 1)
        meta = jnp.where(lane == 0, token // 256, jnp.where(lane == 1, token & 255, 1))
        meta = jnp.where((lane < 3) & live, meta, 0)
        out[rows, width:] = meta.astype(F32).astype(BF)


def turn_kernel(values, out):
    out[...] = values[...].T


def compact_kernel(got, rows_out, meta_out, back_out):
    n = got.shape[0]
    width = got.shape[1] - META
    meta = got[:, width:]
    lower = onehot(iota((n, n), 0) >= iota((n, n), 1))
    running = jnp.dot(lower, meta, preferred_element_type=F32)[:, 2:3]
    live = meta.astype(F32)[:, 2:3]
    spare = ROWS - running[n - 1 : n, :]
    target = jnp.where(live > 0.5, running - 1.0 + spare, -1.0)
    back = jnp.where(iota((n, ROWS), 1).astype(F32) == target, 1.0, 0.0)
    back_out[...] = back.astype(BF)
    place = back.T.astype(BF)
    rows_out[...] = jnp.dot(place, got[:, :width], preferred_element_type=F32).astype(BF)
    meta_out[...] = jnp.dot(place, meta, preferred_element_type=F32).astype(BF)


def project_kernel(order, z, meta, gain, cosine, sine, weight, *refs):
    sources, (out, held, xs, sem, xsem) = refs[:-5], refs[-5:]
    width = xs.shape[2]
    n = len(sources)
    for k, x in enumerate(sources):
        pltpu.make_async_copy(x, xs.at[k], xsem.at[k]).start()
    spots = []
    for k, delta in enumerate(order):
        block = (z[0] + delta + n) & (n - 1)
        at = pl.ds(pl.multiple_of(block * width, width), width)
        pltpu.make_async_copy(weight.at[at], held.at[k], sem.at[k]).start()
        spots.append(at)
    total = jnp.zeros((ROWS, 1), F32)
    for k, x in enumerate(sources):
        pltpu.make_async_copy(x, xs.at[k], xsem.at[k]).wait()
        w = xs[k].astype(F32)
        total += jnp.sum(w * w, axis=1, keepdims=True)
    inv = lax.rsqrt(total / (n * width) + EPS)
    acc = jnp.zeros((ROWS, weight.shape[1]), F32)
    for k in range(n):
        normed = (xs[k].astype(F32) * inv * gain[:, spots[k]]).astype(BF)
        pltpu.make_async_copy(weight.at[spots[k]], held.at[k], sem.at[k]).wait()
        acc += jnp.dot(normed, held[k], preferred_element_type=F32)
    scale = 1.0 / math.sqrt(HEAD)
    for h in range(HEADS):
        at = slice(h * HEAD, (h + 1) * HEAD)
        part = acc[:, at]
        turned = part * cosine[...] + pltpu.roll(part, HEAD // 2, 1) * sine[...]
        out[:, at] = (turned * scale).astype(BF)
    out[:, HEADS * HEAD :] = meta[...]


def three(x):
    a = x.astype(BF).astype(F32)
    b = (x - a).astype(BF).astype(F32)
    return a, b, x - a - b


def attend_kernel(n, shard_ids, first_q, second_q, *refs):
    loads = len(refs) > 2 * n
    keys, values = refs[:n], refs[n : 2 * n]
    if loads:
        first_out, second_out, kbuf, vbuf, *scratch, sem = refs[2 * n :]
        for i in range(n):
            pltpu.make_async_copy(keys[i], kbuf.at[i], sem.at[0, i]).start()
            pltpu.make_async_copy(values[i], vbuf.at[i, pl.ds(0, HEAD)], sem.at[1, i]).start()
        vbuf[:, HEAD:, :] = jnp.ones((n, vbuf.shape[1] - HEAD, vbuf.shape[2]), BF)
    else:
        kbuf, vbuf, first_out, second_out, *scratch = refs
    qbuf, place, even, odd, acc, peak, tops, steps = scratch
    tokens = kbuf.shape[1]
    tiles = ROWS // TILE
    side = TILE * HEADS
    big = 2 * side

    def arrive(done, *codes):
        if not loads:
            return done
        upto = done
        for code in codes:
            upto = jnp.maximum(upto, parts(code)[0] + 1)

        def wait(i, _):
            pltpu.make_async_copy(keys[0], kbuf.at[i], sem.at[0, i]).wait()
            pltpu.make_async_copy(values[0], vbuf.at[i, pl.ds(0, HEAD)], sem.at[1, i]).wait()
            return 0

        lax.fori_loop(done, upto, wait, 0)
        return upto

    lane = iota((8, ROWS), 1)
    spots = []
    for c, query in enumerate((first_q, second_q)):
        meta = query[:, HEADS * HEAD :].astype(F32).T
        row_pos = meta[0:1, :] * 256.0 + meta[1:2, :]
        row_pos = jnp.where(meta[2:3, :] > 0.5, row_pos, -1.0)
        spots.append(row_pos)
        wide = jnp.broadcast_to(row_pos, (8, ROWS))
        for t in range(tiles):
            rows = slice(t * TILE, (t + 1) * TILE)
            spot = jnp.zeros((8, ROWS), F32)
            for h in range(HEADS):
                into = slice(c * side + h * TILE, c * side + (h + 1) * TILE)
                qbuf[t, into, :] = query[rows, h * HEAD : (h + 1) * HEAD]
                moved = pltpu.roll(wide, (h * TILE - t * TILE) % ROWS, 1)
                spot = jnp.where((lane >= h * TILE) & (lane < (h + 1) * TILE), moved, spot)
            place[t, :, c * side : (c + 1) * side] = spot.astype(jnp.int32)
    acc[...] = jnp.zeros_like(acc)
    peak[...] = jnp.full_like(peak, NEG)

    def below(limit):
        found = [jnp.sum(jnp.where(p < limit, 1.0, 0.0)).astype(jnp.int32) for p in spots]
        return jnp.minimum(*found), jnp.maximum(*found)

    bounds = []
    for i in range(n):
        start = (shard_ids[i] * tokens).astype(F32)
        bounds.append((below(start)[0], below(start + tokens)[1]))
    count = jnp.int32(1)
    cut_off = count
    steps[0] = n * tiles
    for masked in (True, False):
        for i in range(n):
            least, most = bounds[i]
            for t in range(tiles):
                steps[count] = i * tiles + t
                cut = t * TILE < most
                here = (t >= least // TILE) & (cut if masked else ~cut)
                count += here.astype(jnp.int32)
        if masked:
            cut_off = count
    for k in range(3):
        steps[count + k] = n * tiles
    base = count & 1
    middle = (cut_off - base + 1) // 2

    def parts(code):
        none = code >= n * tiles
        i = jnp.where(none, 0, code // tiles)
        return i, jnp.where(none, 0, code % tiles), none

    span = 2 * HEAD

    def advance(made, into, made_top, used_step, source, top, masked):
        if made is not None:
            i, t, none = parts(made)
            start = jnp.where(none, 1 << 30, shard_ids[i] * tokens)
            rel = place[t] - start - iota((8, big), 0)
            best = jnp.full((8, big), -jnp.inf, F32)
        if used_step is not None:
            ui, ut, _ = parts(used_step)
            before = peak[ut][0:1, :]
            now = jnp.maximum(before, jnp.max(top[...], axis=0, keepdims=True))
            peak[ut] = jnp.broadcast_to(now, (8, big))
            summed = acc[ut] * jnp.exp(before - now)
        for k in range(tokens // span):
            at = slice(k * span, (k + 1) * span)
            if made is not None:
                s = lax.dot_general(
                    kbuf[i, at, :], qbuf[t], (((1,), (1,)), ((), ())), preferred_element_type=F32
                ).reshape(span // 8, 8, big)
                if masked:
                    keep = rel[None] >= 8 * iota((span // 8, 8, big), 0) + k * span
                    s = jnp.where(keep, s, -jnp.inf)
                best = jnp.maximum(best, jnp.max(s, axis=0))
                into[at, :] = s.reshape(span, big)
            if used_step is not None:
                weight = jnp.exp(source[at, :] - now).astype(BF)
                summed += jnp.dot(vbuf[ui, :, at], weight, preferred_element_type=F32)
        if used_step is not None:
            acc[ut] = summed
        if made is not None:
            made_top[...] = best

    def run(done, first, last, masked):
        def pair(j, done):
            a, b, c = steps[base + 2 * j], steps[base + 2 * j + 1], steps[base + 2 * j + 2]
            done = arrive(done, b, c)
            advance(b, odd, tops.at[1], a, even, tops.at[0], masked)
            advance(c, even, tops.at[0], b, odd, tops.at[1], masked)
            return done

        done = arrive(done, steps[base + 2 * first])
        advance(steps[base + 2 * first], even, tops.at[0], None, None, None, masked)
        return lax.fori_loop(first, last, pair, done)

    done = run(jnp.int32(0), 0, middle, True)
    done = run(done, middle, (count - base) // 2, False)
    arrive(done, jnp.int32(n * tiles - 1))

    for c, out in enumerate((first_out, second_out)):
        lanes = slice(c * side, (c + 1) * side)
        for t in range(tiles):
            rows = slice(t * TILE, (t + 1) * TILE)
            numer = acc[t, :HEAD, lanes].T.astype(BF)
            pieces = three(peak[t, 0:1, lanes]) + three(acc[t, HEAD : HEAD + 1, lanes])
            block = jnp.zeros((META, side), F32)
            row = iota((META, side), 0)
            for k, piece in enumerate(pieces):
                block = jnp.where(row == k, piece, block)
            block = block.T
            stats = jnp.zeros((TILE, META), F32)
            for h in range(HEADS):
                out[rows, h * HEAD : (h + 1) * HEAD] = numer[h * TILE : (h + 1) * TILE, :]
                part = block[h * TILE : (h + 1) * TILE, :]
                stats += pltpu.roll(part, 8 * h, 1) if h else part
            out[rows, HEADS * HEAD :] = stats.astype(BF)


def attend(shard_ids, first_q, second_q, all_k, all_v):
    loads = isinstance(all_k, list)
    n = len(all_k) if loads else all_k.shape[0]
    tokens = all_k[0].shape[0]
    big = 2 * TILE * HEADS
    tiles = ROWS // TILE
    held = (
        jax.ShapeDtypeStruct((n, tokens, HEAD), BF),
        jax.ShapeDtypeStruct((n, HEAD + 16, tokens), BF),
    )
    sources = [*all_k, *all_v] if loads else [all_k, all_v]
    return call(
        functools.partial(attend_kernel, n),
        (jax.ShapeDtypeStruct((ROWS, HEADS * HEAD + META), BF),) * 2 + (held if loads else ()),
        [SM, VM, VM] + ([ANY] * (2 * n) if loads else [VM, VM]),
        shard_ids,
        first_q,
        second_q,
        *sources,
        flops=10**10,
        moved=7 * 10**6,
        scratch_shapes=[
            pltpu.VMEM((tiles, big, HEAD), BF),
            pltpu.VMEM((tiles, 8, big), jnp.int32),
            pltpu.VMEM((tokens, big), F32),
            pltpu.VMEM((tokens, big), F32),
            pltpu.VMEM((tiles, HEAD + 16, big), F32),
            pltpu.VMEM((tiles, 8, big), F32),
            pltpu.VMEM((2, 8, big), F32),
            pltpu.SMEM((n * tiles + 8,), jnp.int32),
        ]
        + ([pltpu.SemaphoreType.DMA((2, n))] if loads else []),
    )


def output_kernel(weight, *refs):
    parts, out = refs[:-1], refs[-1]
    peaks, totals = [], []
    for part in parts:
        meta = part[:, HEADS * HEAD :].astype(F32)
        shifted = [meta] + [pltpu.roll(meta, META - c, 1) for c in range(1, 6)]
        peaks.append(shifted[0] + shifted[1] + shifted[2])
        totals.append(shifted[3] + shifted[4] + shifted[5])
    top = functools.reduce(jnp.maximum, peaks)
    fades = [jnp.exp(p - top) for p in peaks]
    denom = sum(f * t for f, t in zip(fades, totals))
    cols = []
    for h in range(HEADS):
        at = slice(h * HEAD, (h + 1) * HEAD)
        col = slice(8 * h, 8 * h + 1)
        numer = sum(f[:, col] * p[:, at].astype(F32) for f, p in zip(fades, parts))
        d = denom[:, col]
        cols.append((numer / jnp.where(d > 0.0, d, 1.0)).astype(BF))
    mixed = jnp.concatenate(cols, axis=1)
    width = out.shape[2]
    for z in range(out.shape[0]):
        out[z] = jnp.dot(
            mixed, weight[:, z * width : (z + 1) * width], preferred_element_type=F32
        ).astype(BF)


def spread_kernel(back, parts, out):
    total = parts[0].astype(F32)
    for z in range(1, parts.shape[0]):
        total += parts[z].astype(F32)
    out[...] = jnp.dot(back[...], total.astype(BF), preferred_element_type=F32).astype(BF)


def unpack_kernel(shards, count, got, out):
    s, count = seq_place(), count[0]
    slots, n = out.shape[0], got.shape[0]
    slot = iota((slots, n), 0)
    source = ((slot + s) & (shards - 1)) * GROUP + slot // shards
    pick = onehot((iota((slots, n), 1) == source) & (slot < count))
    out[...] = jnp.dot(pick, got[...], preferred_element_type=F32).astype(BF)


def shift(n, k):
    return [(i, (i + k) % n) for i in range(n)]


def body(hidden, norm_gain, w_query, w_out, keys, values, cand_count, cand_pos):
    x, y, c = (lax.axis_index(a) for a in SEQ)
    z = lax.axis_index("head")
    nx, ny, nc, nz = (lax.axis_size(a) for a in (*SEQ, "head"))
    shards = nx * ny * nc
    slots = cand_pos.shape[0]
    width = hidden.shape[1]
    lanes = shards * GROUP

    send = call(
        functools.partial(pack_kernel, shards),
        jax.ShapeDtypeStruct((lanes, width + META), BF),
        [SM, VM, VM],
        cand_count,
        cand_pos,
        hidden,
    )
    swap = [(0, 1), (1, 0)]
    keys, values, send = lax.optimization_barrier((keys, values, send))
    values = call(turn_kernel, jax.ShapeDtypeStruct(values.shape[::-1], BF), [VM], values)
    got = lax.all_to_all(send.reshape(shards, GROUP, -1), SEQ, 0, 0, tiled=True)
    got = got.reshape(lanes, -1)
    k_left, v_left = (
        lax.ppermute(a, SEQ[0], shift(nx, 1)) for a in (keys, values)
    )
    k_right, v_right = (
        lax.ppermute(a, SEQ[0], shift(nx, -1)) for a in (keys, values)
    )
    rows, meta, back = call(
        compact_kernel,
        (
            jax.ShapeDtypeStruct((ROWS, width), BF),
            jax.ShapeDtypeStruct((ROWS, META), BF),
            jax.ShapeDtypeStruct((lanes, ROWS), BF),
        ),
        [VM],
        got,
        flops=5 * 10**9,
        moved=10**6,
    )
    up, down = rows, rows
    slices, order = [rows], [0]
    for k in range(1, nz // 2 + 1):
        up = lax.ppermute(up, "head", shift(nz, 1))
        slices.append(up)
        order.append(-k)
        if k < nz // 2:
            down = lax.ppermute(down, "head", shift(nz, -1))
            slices.append(down)
            order.append(k)

    k_far = lax.ppermute(k_left, SEQ[0], shift(nx, 1))
    v_far = lax.ppermute(v_right, SEQ[0], shift(nx, -1))
    near_k, near_v = [keys, k_left, k_right, k_far], [values, v_left, v_right, v_far]
    all_k = near_k + [lax.ppermute(a, SEQ[2], swap) for a in near_k[:3]]
    all_v = near_v + [lax.ppermute(a, SEQ[2], swap) for a in near_v[:3]]
    all_k.append(lax.ppermute(k_far, SEQ[2], swap))
    all_v.append(lax.ppermute(v_far, SEQ[2], swap))
    places = [((x + d) % nx, cc) for cc in (c, 1 - c) for d in (0, nx - 1, 1, 2)]
    shard_ids = jnp.stack([(px * ny + y) * nc + pc for px, pc in places]).astype(jnp.int32)

    half = HEAD // 2
    freq = jnp.exp(-math.log(ROPE_BASE) * 2.0 * jnp.arange(half, dtype=F32) / HEAD)
    meta_f = meta[:, :2].astype(F32)
    angle = (meta_f[:, 0:1] * 256.0 + meta_f[:, 1:2]) * freq[None, :]
    cosine, sine = jnp.cos(angle), jnp.sin(angle)
    cosine = jnp.concatenate([cosine, cosine], axis=1)
    sine = jnp.concatenate([-sine, sine], axis=1)

    w_query = pltpu.with_memory_space_constraint(w_query, pltpu.HBM)
    slices[:-1] = [pltpu.with_memory_space_constraint(a, pltpu.HBM) for a in slices[:-1]]
    back = pltpu.with_memory_space_constraint(back, pltpu.HBM)
    query = call(
        functools.partial(project_kernel, tuple(order)),
        jax.ShapeDtypeStruct((ROWS, HEADS * HEAD + META), BF),
        [SM, VM, VM, VM, VM, HB] + [HB] * (nz - 1) + [ANY],
        z.reshape(1).astype(jnp.int32),
        meta,
        norm_gain.reshape(1, -1),
        cosine,
        sine,
        w_query,
        *slices,
        scratch_shapes=[
            pltpu.VMEM((nz, width, w_query.shape[1]), BF),
            pltpu.VMEM((nz, ROWS, width), BF),
            pltpu.SemaphoreType.DMA((nz,)),
            pltpu.SemaphoreType.DMA((nz,)),
        ],
    )

    asked = [lax.ppermute(query, SEQ[1], shift(ny, k)) for k in (1, ny - 1)]
    far = lax.ppermute(query, SEQ[1], shift(ny, 2))
    ra, rb, kbuf, vbuf = attend(shard_ids, *asked, all_k, all_v)
    query, far, ra, rb = lax.optimization_barrier((query, far, ra, rb))
    ra = lax.ppermute(ra, SEQ[1], shift(ny, -1))
    rb = lax.ppermute(rb, SEQ[1], shift(ny, 1))
    own, rc = attend(shard_ids, query, far, kbuf, vbuf)
    parts = [own, ra, rb, lax.ppermute(rc, SEQ[1], shift(ny, -2))]

    partial = call(
        output_kernel,
        jax.ShapeDtypeStruct((nz, ROWS, width), BF),
        [VM] * (1 + ny),
        w_out,
        *parts,
    )
    arrived = lax.all_to_all(partial, "head", 0, 0, tiled=True)
    to_send = call(
        spread_kernel, jax.ShapeDtypeStruct((lanes, width), BF), [VM, VM], back, arrived
    )
    returned = lax.all_to_all(to_send.reshape(shards, GROUP, width), SEQ, 0, 0, tiled=True)
    return call(
        functools.partial(unpack_kernel, shards),
        jax.ShapeDtypeStruct((slots, width), BF),
        [SM, VM],
        cand_count,
        returned.reshape(lanes, width),
    )


def solution(mesh):
    split = Mesh(
        mesh.devices.reshape(4, 4, 2, mesh.shape["head"]), ("seq_0", "seq_1", "seq_2", "head")
    )
    placed = (
        P(SEQ, "head"),
        P(),
        P(None, "head"),
        P("head", None),
        P(SEQ, "head"),
        P(SEQ, "head"),
        P(SEQ),
        P(SEQ),
    )

    return jax.shard_map(
        body, mesh=split, in_specs=placed, out_specs=P(SEQ, "head"), check_vma=False
    )
```
